32 devices in a mesh: occ: 4 (over x, core), vir: 8 (over z, y).
Axes of the slice: x: 2, y: 2, z: 4, core: 2. Of those that a mesh axis runs over, the one named last changes fastest.
Arguments:
- amps: bfloat16 [4096, 3072], P('occ', 'vir'), may hold values from -6 to 6
- ints: bfloat16 [3072, 4096], P(None, 'vir'), may hold values from -0.109375 to 0.109375
- amp_mask: int32 [128, 6], P('occ'), may hold values 0 or 1
- keep_mask: int32 [128, 8], P('occ', 'vir'), may hold values 0 or 1
- owners: int32 [128, 1], P('occ'), may hold values from 0 to 3; in each aligned block of 32 rows (0 to 31, 32 to 63, ...) at most 16 rows name the same one
- occ_energy: bfloat16 [4096], P('occ'), may hold values from -2 to -0.5
- vir_energy: float32 [4096], P('vir'), may hold values from 0.5 to 3
- mix: bfloat16 [4, 32, 32], P('occ'), may hold values from -4 to 4
Outputs:
- owned: bfloat16 [256, 32, 4096], P('occ', None, 'vir')
The draws below stay inside these ranges and needn't reach their ends.
Inputs may be any that keep to these rules, and one draw needn't show every extreme that they name: `owners`: in the row tiles of one index of occ no owner appears more than 16 times; in every draw some owner appears exactly 16 times in some device's tiles.
All inputs are finite; a program needn't handle non-finite values. No bound on the sum of `amp_mask` or of `keep_mask` on one device may be relied on, other than what follows from the above.
Results may differ from the reference program's by a relative error of at most 0.0049.
Values may be sent and summed in bfloat16 or wider, within the bound.
A program may use at most 64 MiB of HBM per device.

```python
import math
import jax
import jax.numpy as jnp
import numpy as np

TILE = 512
KT = 6
RT = 32
TILES_DEV = 32
COL_DEV = 512
K = 3072
ROW_TILES = 128
ROWS = 4096
COLS = 4096
OWNERS = 4
CAP = 16
SLOTS = 256
N_VIR = 8


def draw_mix(key, part):
    noise = jax.random.normal(key, (OWNERS, RT, RT), jnp.float32)
    noise = jnp.clip(noise, -5.0, 5.0)
    return (jnp.eye(RT, dtype=jnp.float32)[None] + 0.6 * noise / math.sqrt(RT)).astype(jnp.bfloat16)


def set_ends(entries, own_key, least, largest):
    place = [jax.random.randint(jax.random.fold_in(own_key, axis), (), 0, length) for axis, length in enumerate(entries.shape)]
    widest = entries.shape.index(max(entries.shape))
    next_to = place[:widest] + [(place[widest] + 1) % entries.shape[widest]] + place[widest + 1:]
    return entries.at[tuple(place)].set(least).at[tuple(next_to)].set(largest)


def steps_of(rng, extent, pieces, least, top_value):
    def one(dim, blocks):
        draws = jax.random.uniform(jax.random.fold_in(jax.random.fold_in(rng, 6), dim), (blocks,), jnp.float32, least / len(pieces), top_value / len(pieces))
        return jnp.repeat(jnp.exp(draws), extent[dim] // blocks).reshape((-1,) + (1,) * (len(extent) - dim - 1))

    factor_of = one(*pieces[0])
    for cut in pieces[1:]:
        factor_of = factor_of * one(*cut)
    return factor_of


def routed_block(rng, own, number, rows, number_of, top, limit, slope):
    order = jax.random.permutation(rng, number_of)
    heavy_load, common = portions_of(number_of, rows * top, limit, slope, True), portions_of(number_of, rows * top, limit, slope, False)
    places = jnp.arange(number_of)

    def named(sizes, turn):
        used = int((sizes > 0).sum())
        fixed = max(1, used // 4)
        moved = fixed + (places - fixed + turn * (used - fixed)) % max(1, number_of - fixed)
        return jnp.zeros((number_of,), jnp.int32).at[order[jnp.where(places < fixed, places, moved)]].set(jnp.asarray(sizes, jnp.int32))

    sizes = jnp.where(number % 4 == 0, named(heavy_load, number // 4), named(common, number - number // 4 - 1))
    mixed = jax.random.permutation(jax.random.fold_in(own, 3), number_of)
    giver, receiver = mixed[0:number_of // 2 * 2:2], mixed[1:number_of // 2 * 2:2]
    margin = jnp.minimum(sizes[giver] - 1, limit - sizes[receiver]) // 2
    margin = jnp.where((giver == order[0]) | (receiver == order[0]) | (sizes[receiver] == 0), 0, jnp.maximum(margin, 0))
    moved = jax.random.randint(jax.random.fold_in(own, 4), (number_of // 2,), 0, 1 << 20) % (margin + 1)
    sizes = sizes.at[giver].add(-moved).at[receiver].add(moved)
    members = jnp.searchsorted(jnp.cumsum(sizes), jnp.arange(rows * top), side="right").astype(jnp.int32)
    table = members.reshape(top, rows).T
    table = table[jax.random.permutation(jax.random.fold_in(own, 1), rows)]
    turn = jax.random.randint(jax.random.fold_in(own, 2), (rows, 1), 0, top)
    return jnp.take_along_axis(table, (jnp.arange(top)[None, :] + turn) % top, axis=1)


def portions_of(amount, total, bound, slope, full):
    loads = [(1 << 20) // math.isqrt(grade ** slope) + 1 for grade in range(1, amount + 1)]
    largest = bound if full else min(bound, max(-(-total // amount), total * loads[0] // sum(loads)))
    least = 1 if total - largest >= amount - 1 else 0
    holding, rest = [largest] + [least] * (amount - 1), total - largest - least * (amount - 1)
    while rest > 0:
        movable = [i for i in range(1, amount) if holding[i] < largest] or [i for i in range(1, amount) if holding[i] < bound]
        whole, left = sum([loads[i] for i in movable]), rest
        for i in movable:
            extra = min(bound - holding[i], max(1, left * loads[i] // whole), rest)
            holding[i] = holding[i] + extra
            rest = rest - extra
    return np.array(holding)


def centred(own_key, extent, deviation, limit, shards=(), held_as=jnp.bfloat16):
    values = deviation * jax.random.normal(own_key, extent, jnp.float32)
    if shards:
        values = values * steps_of(own_key, extent, shards, -0.22, 0.18)
    return jnp.clip(values, -limit, limit).astype(held_as)


def setup_inputs(seed: int = 0) -> dict:
    keys = jax.random.split(jax.random.key(seed), 9)
    amps = centred(keys[0], (ROWS, K), 1.0, 6.0, ((0, 4), (1, 8)))
    ints = centred(keys[1], (K, COLS), K ** -0.5, 0.109375, ((1, 8),))
    amp_mask = set_ends((jax.random.randint(keys[2], (ROW_TILES, KT), 0, 3) < 2).astype(jnp.int32), jax.random.fold_in(keys[2], 1), 0, 1)
    keep_mask = set_ends((jax.random.randint(keys[3], (ROW_TILES, N_VIR), 0, 4) < 3).astype(jnp.int32), jax.random.fold_in(keys[3], 1), 0, 1)
    owners_keys = jax.random.split(jax.random.fold_in(keys[4], 1), ROW_TILES // TILES_DEV)
    owners_turns = jax.random.permutation(jax.random.fold_in(keys[4], 3), ROW_TILES // TILES_DEV)
    owners = jax.vmap(lambda own, number: routed_block(jax.random.fold_in(keys[4], 2), own, number, TILES_DEV, OWNERS, 1, CAP, 2))(owners_keys, owners_turns).reshape((ROW_TILES, 1))
    occ_energy = jnp.clip(-2.0 + 1.5 * jax.random.uniform(keys[5], (ROWS,), jnp.float32) ** steps_of(keys[5], (ROWS,), ((0, 4),), -0.2, 0.2), -2.0, -0.5).astype(jnp.bfloat16)
    vir_energy = jnp.clip(0.5 + 2.5 * jax.random.uniform(keys[6], (COLS,), jnp.float32) ** steps_of(keys[6], (COLS,), ((0, 8),), -0.2, 0.2), 0.5, 3.0)
    mix = draw_mix(jax.random.fold_in(keys[8], 71), 0)
    return {"amps": amps, "ints": ints, "amp_mask": amp_mask, "keep_mask": keep_mask, "owners": owners, "occ_energy": occ_energy, "vir_energy": vir_energy, "mix": mix}


def reference(amps, ints, amp_mask, keep_mask, owners, occ_energy, vir_energy, mix):
    k_tile = jnp.arange(K) // TILE
    amp_cols = amp_mask.astype(jnp.float32)[:, k_tile]
    amp_full = jnp.repeat(amp_cols, RT, axis=0)
    masked = (amps.astype(jnp.float32) * amp_full).astype(jnp.bfloat16)
    ladder = jnp.dot(masked, ints, preferred_element_type=jnp.float32).astype(jnp.bfloat16)
    keep_full = jnp.repeat(jnp.repeat(keep_mask.astype(jnp.float32), RT, axis=0), COL_DEV, axis=1)
    kept = (ladder.astype(jnp.float32) * keep_full).astype(jnp.bfloat16)
    tiles = kept.reshape(ROW_TILES, RT, COLS)
    destination = owners[:, 0]
    weights = mix[destination].astype(jnp.float32)
    mixed_rows = jnp.einsum("tij,tjc->tic", weights, tiles.astype(jnp.float32))
    denominator = vir_energy[None, None, :] - occ_energy.astype(jnp.float32).reshape(ROW_TILES, RT)[:, :, None]
    update = (mixed_rows / denominator).astype(jnp.bfloat16)
    grouped = destination.reshape(OWNERS, TILES_DEV)
    same_owner = grouped[:, :, None] == grouped[:, None, :]
    earlier = jnp.arange(TILES_DEV)[:, None] > jnp.arange(TILES_DEV)[None, :]
    position = jnp.sum((same_owner & earlier[None]).astype(jnp.int32), axis=2).reshape(-1)
    source = (jnp.arange(ROW_TILES) // TILES_DEV).astype(jnp.int32)
    slot_index = (destination * (OWNERS * CAP) + source * CAP + position).astype(jnp.int32)
    owned = jnp.zeros((SLOTS, RT, COLS), jnp.bfloat16).at[slot_index].set(update)
    return owned
```

```python
import functools

import jax
import jax.numpy as jnp
from jax import lax
from jax.experimental import pallas as pl
from jax.experimental.pallas import tpu as pltpu
from jax.sharding import PartitionSpec as P

MESH = pl.DeviceIdType.MESH


def ladder_kernel(
    cfg, amps, ints, amp_mask, keep, own_s, own_v, occ, vir, mix, keep_v, out,
    gath, ints_own, ints_end, masked, occ_col, tiles, tiles_end, mix_all, own_all, own_tab, nxt,
    vir_end, keep_land, keep_end,
    lsem, rsem_g, ssem_g, rsem_b, ssem_b, ssem_bx, ssem_bc, rsem_t, ssem_c, ssem_t, ssem_r,
    rsem_o, ssem_o, rsem_s, ssem_s,
):
    no, nv, td, tr, chunk_tiles, k_tile, ahead, lead, nb = cfg
    ng, nz = no // 2, nv // 2
    rows, kw = amps.shape
    depth, cols = ints.shape
    cr = chunk_tiles * tr
    nc = rows // cr
    cap = out.shape[0] // no
    share = depth // no
    part = share // nb
    o, v = lax.axis_index("occ"), lax.axis_index("vir")
    g, c = o // 2, o % 2
    z, y = v // 2, v % 2
    mate = z * 2 + (1 - y)
    is_end = (z == 0) | (z == nz - 1)
    inner = jnp.logical_not(is_end)
    has_end = (z == 1) | (z == nz - 2)
    go_up = (z >= 1) & (z < nz - 2)
    go_down = (z > 1) & (z <= nz - 2)
    partner = {"occ": g * 2 + (1 - c), "vir": v}
    side = {"occ": o, "vir": mate}
    above = {"occ": o, "vir": (z + 1) * 2 + y}
    below = {"occ": o, "vir": (z - 1) * 2 + y}
    inward = {"occ": o, "vir": jnp.where(z == 0, 1, nz - 2) * 2 + y}
    outward = {"occ": o, "vir": jnp.where(z == 1, 0, nz - 1) * 2 + y}

    load_own = pltpu.make_async_copy(own_v, own_all.at[o], lsem.at[0])
    load_mix = pltpu.make_async_copy(mix.at[0], mix_all.at[o], lsem.at[1])
    load_ints = pltpu.make_async_copy(ints, ints_own, lsem.at[2])
    load_amps = pltpu.make_async_copy(amps, gath.at[v], lsem.at[3])
    load_own.start()
    load_mix.start()

    @pl.when(inner)
    def _():
        load_amps.start()
        load_ints.start()

    barrier = pltpu.get_barrier_semaphore()

    def greet(device):
        pl.semaphore_signal(barrier, inc=1, device_id=device, device_id_type=MESH)

    for d in range(1, no):
        greet({"occ": (o + d) % no, "vir": v})
    greet(side)

    @pl.when(z < nz - 1)
    def _():
        greet(above)

    @pl.when(z > 0)
    def _():
        greet(below)

    both = jnp.where(z < nz - 1, 1, 0) + jnp.where(z > 0, 1, 0)
    pl.semaphore_wait(barrier, no + both)

    def crosses_early(i):
        return (i % 3 != 0) | (i == nc - 1)

    early = sum(1 for i in range(nc) if i % 3 != 0 or i == nc - 1) * cr

    def piece(src, slot, i, send_sem, device):
        window = pl.ds(pl.multiple_of(i * cr, cr), cr)
        return pltpu.make_async_remote_copy(
            src_ref=src.at[window], dst_ref=gath.at[slot, window], send_sem=send_sem,
            recv_sem=rsem_g.at[slot, i], device_id=device, device_id_type=MESH,
        )

    def arrive(slot, i):
        piece(gath.at[slot], slot, i, ssem_g.at[2, 0], side).wait_recv()

    def small(d, o2):
        peer = {"occ": (o + d) % no, "vir": v}
        return [
            pltpu.make_async_remote_copy(
                src_ref=own_v, dst_ref=own_all.at[o2], send_sem=ssem_o.at[0, d],
                recv_sem=rsem_o.at[0, o2], device_id=peer, device_id_type=MESH),
            pltpu.make_async_remote_copy(
                src_ref=mix.at[0], dst_ref=mix_all.at[o2], send_sem=ssem_o.at[1, d],
                recv_sem=rsem_o.at[1, o2], device_id=peer, device_id_type=MESH),
        ]

    def end_rows():
        return [
            pltpu.make_async_remote_copy(
                src_ref=vir, dst_ref=vir_end, send_sem=ssem_s.at[0], recv_sem=rsem_s.at[0],
                device_id=inward, device_id_type=MESH),
            pltpu.make_async_remote_copy(
                src_ref=keep_v, dst_ref=keep_land, send_sem=ssem_s.at[1], recv_sem=rsem_s.at[1],
                device_id=inward, device_id_type=MESH),
        ]

    def table():
        for d in range(1, no):
            for copy in small(d, (o + d) % no):
                copy.wait_recv()
        load_own.wait()
        load_mix.wait()
        copy = pltpu.make_async_copy(own_all, own_tab, lsem.at[4])
        copy.start()
        copy.wait()

        def scan_source(s, carry):
            nxt[s, td] = td

            def back(n, following):
                t = td - 1 - n
                following = jnp.where(own_tab[s, 0, t] == o, t, following)
                nxt[s, t] = following
                return following

            lax.fori_loop(0, td, back, jnp.int32(td))
            return carry

        lax.fori_loop(0, no, scan_source, 0)

    def group_of(d):
        return ((g + d) % ng) * 2

    def tile_piece(o2, i, send_sem, device):
        window = pl.ds(i * chunk_tiles, chunk_tiles)
        return pltpu.make_async_remote_copy(
            src_ref=tiles.at[o2, window], dst_ref=tiles.at[o2, window], send_sem=send_sem,
            recv_sem=rsem_t.at[o2, i], device_id=device, device_id_type=MESH,
        )

    def back_piece(i):
        window = pl.ds(i * chunk_tiles, chunk_tiles)
        return pltpu.make_async_remote_copy(
            src_ref=tiles_end.at[window], dst_ref=tiles.at[o, window], send_sem=ssem_r.at[0],
            recv_sem=rsem_t.at[o, i], device_id=outward, device_id_type=MESH,
        )

    def share_out(i):
        for d in range(1, ng):
            tile_piece(o, i, ssem_t.at[d], {"occ": group_of(d) + c, "vir": v}).start()
        tile_piece(o, i, ssem_c.at[0], partner).start()

    def hand_on(i):
        for d in range(1, ng):
            o2 = group_of(d) + c
            tile_piece(o2, i, ssem_c.at[d], partner).wait_recv()
            tile_piece(o2, i, ssem_c.at[d], partner).start()

    def block(q, p):
        return pl.ds(pl.multiple_of(q * share + p * part, part), part)

    def ints_piece(src, q, p, send_sem, device):
        return pltpu.make_async_remote_copy(
            src_ref=src.at[block(q, p)], dst_ref=ints_end.at[block(q, p)], send_sem=send_sem,
            recv_sem=rsem_b.at[q, p], device_id=device, device_id_type=MESH,
        )

    def ints_arrive(q, p):
        ints_piece(ints_end, q, p, ssem_b.at[0], partner).wait_recv()

    @pl.when(is_end)
    def _():
        for copy in end_rows():
            copy.start()

        def cross(i, carry):
            @pl.when(crosses_early(i))
            def _():
                piece(amps, v, i, ssem_g.at[2, v], side).start()

            return carry

        lax.fori_loop(0, nc, cross, 0)

        def send_ints(p):
            ints_piece(ints, o, p, ssem_b.at[0], inward).start()

        def send_amps(i):
            piece(amps, v, i, ssem_g.at[0, v], inward).start()

            @pl.when(crosses_early(i))
            def _():
                arrive(mate, i)
                piece(gath.at[mate], mate, i, ssem_g.at[0, mate], inward).start()

        for p in range(nb - 1):
            send_ints(p)
        for d in range(1, no):
            for copy in small(d, o):
                copy.start()
        send_amps(0)
        send_ints(nb - 1)

        def rest(i, carry):
            send_amps(i)
            return carry

        lax.fori_loop(1, nc, rest, 0)
        table()

        def pass_on(i, carry):
            tile_piece(o, i, ssem_c.at[0], partner).wait_recv()
            share_out(i)

            @pl.when(i > 0)
            def _():
                hand_on(i - 1)

            return carry

        lax.fori_loop(0, nc, pass_on, 0)
        hand_on(nc - 1)

    def mask_rows(i):
        first = pl.multiple_of(i * cr, cr)
        for slot in range(nv):
            rows_in = gath[slot, pl.ds(first, cr), :]
            column = slot * kw + lax.broadcasted_iota(jnp.int32, (1, kw), 1)
            low, high = slot * kw // k_tile, ((slot + 1) * kw - 1) // k_tile
            for n in range(chunk_tiles):
                t = i * chunk_tiles + n
                flag = jnp.full((1, kw), amp_mask[low, t].astype(jnp.float32))
                for s in range(low + 1, high + 1):
                    flag = jnp.where(column >= s * k_tile, amp_mask[s, t].astype(jnp.float32), flag)
                flag = jnp.broadcast_to(flag, (tr, kw)).astype(jnp.bfloat16)
                masked[slot, n * tr:(n + 1) * tr, :] = rows_in[n * tr:(n + 1) * tr] * flag

    def ladder_of(right):
        if kw % 128 == 0:
            left = jnp.concatenate([masked[slot] for slot in range(nv)], axis=1)
            return jnp.dot(left, right[...], preferred_element_type=jnp.float32)
        total = jnp.zeros((cr, cols), jnp.float32)
        for slot in range(nv):
            total += jnp.dot(
                masked[slot], right[slot * kw:(slot + 1) * kw, :], preferred_element_type=jnp.float32)
        return total

    def update(i, right, keep_row, vir_row, store):
        ladder = ladder_of(right).astype(jnp.bfloat16)
        for n in range(chunk_tiles):
            t = i * chunk_tiles + n
            kept = ladder[n * tr:(n + 1) * tr] * keep_row[0, t].astype(jnp.float32).astype(jnp.bfloat16)
            mixed = jnp.dot(mix_all[own_s[0, t]], kept, preferred_element_type=jnp.float32)
            energy = occ_col[pl.ds(pl.multiple_of(t * tr, tr), tr), :]
            denominator = vir_row[...] - jnp.concatenate([energy] * (cols // 128), axis=1)
            store(t, (mixed / denominator).astype(jnp.bfloat16))

    @pl.when(inner)
    def _():
        def send_own(i):
            @pl.when(go_up)
            def _():
                piece(amps, v, i, ssem_g.at[0, v], above).start()

            @pl.when(go_down)
            def _():
                piece(amps, v, i, ssem_g.at[1, v], below).start()

        def send_side(i):
            piece(amps, v, i, ssem_g.at[2, v], side).start()

        for i in range(min(ahead, nc)):
            send_side(i)

        def all_own(i, carry):
            send_own(i)
            return carry

        lax.fori_loop(0, nc, all_own, 0)
        for d in range(1, no):
            for copy in small(d, o):
                copy.start()

        lanes = occ.shape[1]
        for r in range(occ.shape[0]):
            row = jnp.broadcast_to(occ[...].astype(jnp.float32)[r:r + 1], (128, lanes))
            occ_col[r * lanes:(r + 1) * lanes, :] = jnp.transpose(row)

        def within(i, body):
            @pl.when((i >= 0) & (i < nc))
            def _():
                body(i)

        def relay(slot, i, up):
            ok, sem, device = (go_up, 0, above) if up else (go_down, 1, below)

            @pl.when(ok)
            def _():
                piece(gath.at[slot], slot, i, ssem_g.at[sem, slot], device).start()

        def from_inner(j, i):
            for near, up in ((z - j, True), (z + j, False)):
                @pl.when((near >= 1) & (near <= nz - 2))
                def _():
                    slot = near * 2 + y
                    arrive(slot, i)
                    relay(slot, i, up)
                    piece(gath.at[slot], slot, i, ssem_g.at[2, slot], side).start()

        def from_end(j, i):
            for near, end, up in ((z - j, 0, True), (z + j, nz - 1, False)):
                @pl.when(near == end)
                def _():
                    slot = end * 2 + y
                    other = end * 2 + (1 - y)
                    arrive(slot, i)
                    relay(slot, i, up)

                    @pl.when(crosses_early(i))
                    def _():
                        arrive(other, i)
                        relay(other, i, up)

                    @pl.when(jnp.logical_not(crosses_early(i)))
                    def _():
                        piece(gath.at[slot], slot, i, ssem_g.at[2, slot], side).start()

        def from_outward(p):
            @pl.when(has_end)
            def _():
                ints_arrive(o, p)
                for d in range(1, ng):
                    ints_piece(ints_end, o, p, ssem_bx.at[d], {"occ": group_of(d) + c, "vir": v}).start()
                ints_piece(ints_end, o, p, ssem_bc.at[0], partner).start()

        def ints_on(p):
            @pl.when(has_end)
            def _():
                for d in range(1, ng):
                    ints_arrive(group_of(d) + c, p)
                    ints_piece(ints_end, group_of(d) + c, p, ssem_bc.at[d], partner).start()

        def ints_last():
            for p in range(nb):
                for d in range(ng):
                    ints_arrive(group_of(d) + (1 - c), p)
            for copy in end_rows():
                copy.wait_recv()
            copy = pltpu.make_async_copy(keep_land, keep_end, lsem.at[5])
            copy.start()
            copy.wait()

        def finish(i):
            for zz in range(1, nz - 1):
                arrive(zz * 2 + (1 - y), i)

            @pl.when(jnp.logical_not(crosses_early(i)))
            def _():
                arrive(1 - y, i)
                arrive((nz - 1) * 2 + (1 - y), i)

            @pl.when(i == 0)
            def _():
                load_ints.wait()
                load_amps.wait()
                table()

            mask_rows(i)

            @pl.when(has_end)
            def _():
                @pl.when(i == 0)
                def _():
                    ints_last()

                def store_end(t, value):
                    tiles_end[t] = value

                update(i, ints_end, keep_end, vir_end, store_end)
                back_piece(i).start()

            def store_own(t, value):
                tiles[o, t] = value

            update(i, ints_own, keep, vir, store_own)
            share_out(i)

        lag = nz - 3

        def step(s, carry):
            if nz == 4:
                n = jnp.where(s < 5, s, jnp.where(s % 2 == 0, 2 + s // 2, nc + nz))
            else:
                n = s
            within(n + ahead, send_side)
            for j in range(1, nz - 2):
                within(n - (j - 1), functools.partial(from_inner, j))

            @pl.when(s < nb - 1)
            def _():
                from_outward(s)

            @pl.when(s == nb)
            def _():
                from_outward(nb - 1)

            @pl.when((s >= 1) & (s < nb))
            def _():
                ints_on(s - 1)

            e = s - lead
            for j in range(1, nz - 1):
                within(e - (j - 1), functools.partial(from_end, j))

            @pl.when(s == nb)
            def _():
                ints_on(nb - 1)

            within(e - lag, finish)
            within(e - lag - 1, hand_on)
            return carry

        lax.fori_loop(0, nc + lead + lag + 1, step, 0)

    def last(i, carry):
        for d in range(ng):
            tile_piece(group_of(d) + (1 - c), i, ssem_c.at[d], partner).wait_recv()
        return carry

    lax.fori_loop(0, nc, last, 0)

    def source(s, carry):
        def slot(k, position):
            t = nxt[s, position]
            tile = tiles[s, jnp.minimum(t, td - 1)]
            out[s * cap + k] = jnp.where(t < td, tile, jnp.zeros_like(tile))
            return jnp.minimum(t + 1, td)

        lax.fori_loop(0, cap, slot, jnp.int32(0))
        return carry

    lax.fori_loop(0, no, source, 0)

    def sent(whole, send_sem, recv_sem):
        pltpu.make_async_remote_copy(
            src_ref=whole, dst_ref=whole, send_sem=send_sem, recv_sem=recv_sem,
            device_id=partner, device_id_type=MESH).wait_send()

    def sent_rows(count, direction, slot):
        if count:
            sent(gath.at[0, pl.ds(0, count)], ssem_g.at[direction, slot], rsem_g.at[0, 0])

    @pl.when(is_end)
    def _():
        sent_rows(early, 2, v)
        sent_rows(rows, 0, v)
        sent_rows(early, 0, mate)
        sent(ints_end.at[pl.ds(0, share)], ssem_b.at[0], rsem_b.at[0, 0])
        for copy in end_rows():
            copy.wait_send()

    @pl.when(inner)
    def _():
        sent_rows(rows, 2, v)
        for zz in range(nz):
            is_far = zz in (0, nz - 1)
            for direction, ok, along in ((0, go_up, zz <= z), (1, go_down, zz >= z)):
                @pl.when(ok & along)
                def _():
                    sent_rows(rows, direction, zz * 2 + y)
                    if is_far:
                        sent_rows(early, direction, zz * 2 + (1 - y))

            @pl.when(zz != z)
            def _():
                sent_rows(rows - early if is_far else rows, 2, zz * 2 + y)

        @pl.when(has_end)
        def _():
            for d in range(ng):
                whole = ints_end.at[pl.ds(0, share)]
                sent(whole, ssem_bc.at[d], rsem_b.at[0, 0])
                if d:
                    sent(whole, ssem_bx.at[d], rsem_b.at[0, 0])
            sent(tiles_end, ssem_r.at[0], rsem_t.at[0, 0])

    for d in range(ng):
        sent(tiles.at[d], ssem_c.at[d], rsem_t.at[0, 0])
        if d:
            sent(tiles.at[d], ssem_t.at[d], rsem_t.at[0, 0])
    for d in range(1, no):
        for copy in small(d, o):
            copy.wait_send()


def shards(no, nv, amps, ints, amp_mask, keep_mask, owners, occ_energy, vir_energy, mix):
    td, k_tiles = amp_mask.shape
    rows, kw = amps.shape
    tr = rows // td
    cols = ints.shape[1]
    k_tile = ints.shape[0] // k_tiles
    cap = max(2, 2 * td // no)
    chunk_tiles = max(1, min(td, 128 // tr))
    nc = td // chunk_tiles
    ahead, lead, nb = 2, 3, 4
    cfg = (no, nv, td, tr, chunk_tiles, k_tile, ahead, lead, nb)
    smem = pl.BlockSpec(memory_space=pltpu.SMEM)
    vmem = pl.BlockSpec(memory_space=pltpu.VMEM)
    hbm = pl.BlockSpec(memory_space=pl.ANY)
    ng = no // 2
    own = owners.reshape(1, td)
    keep = keep_mask.reshape(1, td)
    dma = pltpu.SemaphoreType.DMA
    return pl.pallas_call(
        functools.partial(ladder_kernel, cfg),
        out_shape=jax.ShapeDtypeStruct((no * cap, tr, cols), jnp.bfloat16),
        in_specs=[hbm, hbm, smem, smem, smem, vmem, vmem, vmem, vmem, vmem],
        out_specs=vmem,
        scratch_shapes=[
            pltpu.VMEM((nv, rows, kw), jnp.bfloat16),
            pltpu.VMEM(ints.shape, jnp.bfloat16),
            pltpu.VMEM(ints.shape, jnp.bfloat16),
            pltpu.VMEM((nv, chunk_tiles * tr, kw), jnp.bfloat16),
            pltpu.VMEM((rows, 128), jnp.float32),
            pltpu.VMEM((no, td, tr, cols), jnp.bfloat16),
            pltpu.VMEM((td, tr, cols), jnp.bfloat16),
            pltpu.VMEM((no, tr, tr), jnp.bfloat16),
            pltpu.VMEM((no, 1, td), jnp.int32),
            pltpu.SMEM((no, 1, td), jnp.int32),
            pltpu.SMEM((no, td + 1), jnp.int32),
            pltpu.VMEM((1, cols), jnp.float32),
            pltpu.VMEM((1, td), jnp.int32),
            pltpu.SMEM((1, td), jnp.int32),
            dma((6,)),
            dma((nv, nc)),
            dma((3, nv)),
            dma((no, nb)),
            dma((1,)),
            dma((ng,)),
            dma((ng,)),
            dma((no, nc)),
            dma((ng,)),
            dma((ng,)),
            dma((1,)),
            dma((2, no)),
            dma((2, no)),
            dma((2,)),
            dma((2,)),
        ],
        compiler_params=pltpu.CompilerParams(
            collective_id=0, has_side_effects=True, vmem_limit_bytes=60 * 1024 * 1024
        ),
    )(
        amps, ints, amp_mask.T, keep, own, own,
        occ_energy.reshape(rows // 128, 128),
        vir_energy.reshape(1, cols), mix, keep,
    )


def solution(mesh):
    in_specs = (
        P("occ", "vir"),
        P(None, "vir"),
        P("occ", None),
        P("occ", "vir"),
        P("occ", None),
        P("occ"),
        P("vir"),
        P("occ", None, None),
    )
    body = functools.partial(shards, mesh.shape["occ"], mesh.shape["vir"])
    return jax.shard_map(
        body, mesh=mesh, in_specs=in_specs, out_specs=P("occ", None, "vir"), check_vma=False
    )
```

```python
import functools

import jax
import jax.numpy as jnp
from jax import lax
from jax.experimental import pallas as pl
from jax.experimental.pallas import tpu as pltpu
from jax.sharding import PartitionSpec as P

MESH = pl.DeviceIdType.MESH


def ladder_kernel(
    cfg, amps, ints, amp_mask, keep, own_s, own_v, occ, vir, mix, keep_v, out,
    gath, ints_own, ints_end, masked, occ_col, tiles, tiles_end, mix_all, own_all, own_tab, nxt,
    vir_end, keep_land, keep_end,
    lsem, rsem_g, ssem_g, rsem_b, ssem_b, ssem_bx, ssem_bc, rsem_t, ssem_c, ssem_t, ssem_r,
    rsem_o, ssem_o, rsem_s, ssem_s,
):
    no, nv, td, tr, chunk_tiles, k_tile, ahead, lead, nb, late = cfg
    ng, nz = no // 2, nv // 2
    rows, kw = amps.shape
    depth, cols = ints.shape
    cr = chunk_tiles * tr
    nc = rows // cr
    pt = chunk_tiles // 2
    pr = pt * tr
    np_ = rows // pr
    cap = out.shape[0] // no
    share = depth // no
    part = share // nb
    o, v = lax.axis_index("occ"), lax.axis_index("vir")
    g, c = o // 2, o % 2
    z, y = v // 2, v % 2
    mate = z * 2 + (1 - y)
    is_end = (z == 0) | (z == nz - 1)
    inner = jnp.logical_not(is_end)
    has_end = (z == 1) | (z == nz - 2)
    go_up = (z >= 1) & (z < nz - 2)
    go_down = (z > 1) & (z <= nz - 2)
    partner = {"occ": g * 2 + (1 - c), "vir": v}
    side = {"occ": o, "vir": mate}
    above = {"occ": o, "vir": (z + 1) * 2 + y}
    below = {"occ": o, "vir": (z - 1) * 2 + y}
    inward = {"occ": o, "vir": jnp.where(z == 0, 1, nz - 2) * 2 + y}
    outward = {"occ": o, "vir": jnp.where(z == 1, 0, nz - 1) * 2 + y}

    load_own = pltpu.make_async_copy(own_v, own_all.at[o], lsem.at[0])
    load_mix = pltpu.make_async_copy(mix.at[0], mix_all.at[o], lsem.at[1])
    load_ints = pltpu.make_async_copy(ints, ints_own, lsem.at[2])
    load_amps = pltpu.make_async_copy(amps, gath.at[v], lsem.at[3])
    load_own.start()
    load_mix.start()

    @pl.when(inner)
    def _():
        load_amps.start()
        load_ints.start()

    barrier = pltpu.get_barrier_semaphore()

    def greet(device):
        pl.semaphore_signal(barrier, inc=1, device_id=device, device_id_type=MESH)

    for d in range(1, no):
        greet({"occ": (o + d) % no, "vir": v})
    greet(side)

    @pl.when(z < nz - 1)
    def _():
        greet(above)

    @pl.when(z > 0)
    def _():
        greet(below)

    both = jnp.where(z < nz - 1, 1, 0) + jnp.where(z > 0, 1, 0)
    pl.semaphore_wait(barrier, no + both)

    def crosses_early(i):
        return (i % 3 != 1) | (i >= late)

    early = sum(1 for i in range(np_) if i % 3 != 1 or i >= late) * pr

    def piece(src, slot, i, send_sem, device):
        window = pl.ds(pl.multiple_of(i * pr, pr), pr)
        return pltpu.make_async_remote_copy(
            src_ref=src.at[window], dst_ref=gath.at[slot, window], send_sem=send_sem,
            recv_sem=rsem_g.at[slot, i], device_id=device, device_id_type=MESH,
        )

    def arrive(slot, i):
        piece(gath.at[slot], slot, i, ssem_g.at[2, 0], side).wait_recv()

    def small(d, o2):
        peer = {"occ": (o + d) % no, "vir": v}
        return [
            pltpu.make_async_remote_copy(
                src_ref=own_v, dst_ref=own_all.at[o2], send_sem=ssem_o.at[0, d],
                recv_sem=rsem_o.at[0, o2], device_id=peer, device_id_type=MESH),
            pltpu.make_async_remote_copy(
                src_ref=mix.at[0], dst_ref=mix_all.at[o2], send_sem=ssem_o.at[1, d],
                recv_sem=rsem_o.at[1, o2], device_id=peer, device_id_type=MESH),
        ]

    def end_rows():
        return [
            pltpu.make_async_remote_copy(
                src_ref=vir, dst_ref=vir_end, send_sem=ssem_s.at[0], recv_sem=rsem_s.at[0],
                device_id=inward, device_id_type=MESH),
            pltpu.make_async_remote_copy(
                src_ref=keep_v, dst_ref=keep_land, send_sem=ssem_s.at[1], recv_sem=rsem_s.at[1],
                device_id=inward, device_id_type=MESH),
        ]

    def table():
        for d in range(1, no):
            for copy in small(d, (o + d) % no):
                copy.wait_recv()
        load_own.wait()
        load_mix.wait()
        copy = pltpu.make_async_copy(own_all, own_tab, lsem.at[4])
        copy.start()
        copy.wait()

        def scan_source(s, carry):
            nxt[s, td] = td

            def back(n, following):
                t = td - 1 - n
                following = jnp.where(own_tab[s, 0, t] == o, t, following)
                nxt[s, t] = following
                return following

            lax.fori_loop(0, td, back, jnp.int32(td))
            return carry

        lax.fori_loop(0, no, scan_source, 0)

    def group_of(d):
        return ((g + d) % ng) * 2

    def tile_piece(o2, i, send_sem, device):
        window = pl.ds(i * pt, pt)
        return pltpu.make_async_remote_copy(
            src_ref=tiles.at[o2, window], dst_ref=tiles.at[o2, window], send_sem=send_sem,
            recv_sem=rsem_t.at[o2, i], device_id=device, device_id_type=MESH,
        )

    def back_piece(i):
        window = pl.ds(i * pt, pt)
        return pltpu.make_async_remote_copy(
            src_ref=tiles_end.at[window], dst_ref=tiles.at[o, window], send_sem=ssem_r.at[0],
            recv_sem=rsem_t.at[o, i], device_id=outward, device_id_type=MESH,
        )

    def share_out(i):
        for d in range(1, ng):
            tile_piece(o, i, ssem_t.at[d], {"occ": group_of(d) + c, "vir": v}).start()
        tile_piece(o, i, ssem_c.at[0], partner).start()

    def hand_on(i):
        for d in range(1, ng):
            o2 = group_of(d) + c
            tile_piece(o2, i, ssem_c.at[d], partner).wait_recv()
            tile_piece(o2, i, ssem_c.at[d], partner).start()

    def block(q, p):
        return pl.ds(pl.multiple_of(q * share + p * part, part), part)

    def ints_piece(src, q, p, send_sem, device):
        return pltpu.make_async_remote_copy(
            src_ref=src.at[block(q, p)], dst_ref=ints_end.at[block(q, p)], send_sem=send_sem,
            recv_sem=rsem_b.at[q, p], device_id=device, device_id_type=MESH,
        )

    def ints_arrive(q, p):
        ints_piece(ints_end, q, p, ssem_b.at[0], partner).wait_recv()

    @pl.when(is_end)
    def _():
        for copy in end_rows():
            copy.start()

        def cross(i, carry):
            @pl.when(crosses_early(i))
            def _():
                piece(amps, v, i, ssem_g.at[2, v], side).start()

            return carry

        lax.fori_loop(0, np_, cross, 0)

        def send_ints(p):
            ints_piece(ints, o, p, ssem_b.at[0], inward).start()

        def send_amps(i):
            piece(amps, v, i, ssem_g.at[0, v], inward).start()

            @pl.when(crosses_early(i))
            def _():
                arrive(mate, i)
                piece(gath.at[mate], mate, i, ssem_g.at[0, mate], inward).start()

        for p in range(nb - 1):
            send_ints(p)
        for d in range(1, no):
            for copy in small(d, o):
                copy.start()
        send_amps(0)
        send_ints(nb - 1)

        def rest(i, carry):
            send_amps(i)
            return carry

        lax.fori_loop(1, np_, rest, 0)
        table()

        def pass_on(i, carry):
            tile_piece(o, i, ssem_c.at[0], partner).wait_recv()
            share_out(i)

            @pl.when(i >= 3)
            def _():
                hand_on(i - 3)

            return carry

        lax.fori_loop(0, np_, pass_on, 0)
        for i in range(np_ - 3, np_):
            hand_on(i)

    def mask_rows(i):
        first = pl.multiple_of(i * cr, cr)
        for slot in range(nv):
            rows_in = gath[slot, pl.ds(first, cr), :]
            column = slot * kw + lax.broadcasted_iota(jnp.int32, (1, kw), 1)
            low, high = slot * kw // k_tile, ((slot + 1) * kw - 1) // k_tile
            for n in range(chunk_tiles):
                t = i * chunk_tiles + n
                flag = jnp.full((1, kw), amp_mask[low, t].astype(jnp.float32))
                for s in range(low + 1, high + 1):
                    flag = jnp.where(column >= s * k_tile, amp_mask[s, t].astype(jnp.float32), flag)
                flag = jnp.broadcast_to(flag, (tr, kw)).astype(jnp.bfloat16)
                masked[slot, n * tr:(n + 1) * tr, :] = rows_in[n * tr:(n + 1) * tr] * flag

    def ladder_of(right):
        if kw % 128 == 0:
            left = jnp.concatenate([masked[slot] for slot in range(nv)], axis=1)
            return jnp.dot(left, right[...], preferred_element_type=jnp.float32)
        total = jnp.zeros((cr, cols), jnp.float32)
        for slot in range(nv):
            total += jnp.dot(
                masked[slot], right[slot * kw:(slot + 1) * kw, :], preferred_element_type=jnp.float32)
        return total

    def update(i, right, keep_row, vir_row, store, send):
        ladder = ladder_of(right).astype(jnp.bfloat16)
        for n in range(chunk_tiles):
            t = i * chunk_tiles + n
            kept = ladder[n * tr:(n + 1) * tr] * keep_row[0, t].astype(jnp.float32).astype(jnp.bfloat16)
            mixed = jnp.dot(mix_all[own_s[0, t]], kept, preferred_element_type=jnp.float32)
            energy = occ_col[pl.ds(pl.multiple_of(t * tr, tr), tr), :]
            denominator = vir_row[...] - jnp.concatenate([energy] * (cols // 128), axis=1)
            store(t, (mixed / denominator).astype(jnp.bfloat16))
            if n % pt == pt - 1:
                send(2 * i + n // pt)

    @pl.when(inner)
    def _():
        def send_own(i):
            @pl.when(go_up)
            def _():
                piece(amps, v, i, ssem_g.at[0, v], above).start()

            @pl.when(go_down)
            def _():
                piece(amps, v, i, ssem_g.at[1, v], below).start()

        def send_side(i):
            piece(amps, v, i, ssem_g.at[2, v], side).start()

        for i in range(min(ahead, np_)):
            send_side(i)

        def all_own(i, carry):
            send_own(i)
            return carry

        lax.fori_loop(0, np_, all_own, 0)
        for d in range(1, no):
            for copy in small(d, o):
                copy.start()

        lanes = occ.shape[1]
        for r in range(occ.shape[0]):
            row = jnp.broadcast_to(occ[...].astype(jnp.float32)[r:r + 1], (128, lanes))
            occ_col[r * lanes:(r + 1) * lanes, :] = jnp.transpose(row)

        def within(i, body):
            @pl.when((i >= 0) & (i < np_))
            def _():
                body(i)

        def relay(slot, i, up):
            ok, sem, device = (go_up, 0, above) if up else (go_down, 1, below)

            @pl.when(ok)
            def _():
                piece(gath.at[slot], slot, i, ssem_g.at[sem, slot], device).start()

        def from_inner(j, i):
            for near, up in ((z - j, True), (z + j, False)):
                @pl.when((near >= 1) & (near <= nz - 2))
                def _():
                    slot = near * 2 + y
                    arrive(slot, i)
                    relay(slot, i, up)
                    piece(gath.at[slot], slot, i, ssem_g.at[2, slot], side).start()

        def from_end(j, i):
            for near, end, up in ((z - j, 0, True), (z + j, nz - 1, False)):
                @pl.when(near == end)
                def _():
                    slot = end * 2 + y
                    other = end * 2 + (1 - y)
                    arrive(slot, i)
                    relay(slot, i, up)

                    @pl.when(crosses_early(i))
                    def _():
                        arrive(other, i)
                        relay(other, i, up)

                    @pl.when(jnp.logical_not(crosses_early(i)))
                    def _():
                        piece(gath.at[slot], slot, i, ssem_g.at[2, slot], side).start()

        def from_outward(p):
            @pl.when(has_end)
            def _():
                ints_arrive(o, p)
                for d in range(1, ng):
                    ints_piece(ints_end, o, p, ssem_bx.at[d], {"occ": group_of(d) + c, "vir": v}).start()
                ints_piece(ints_end, o, p, ssem_bc.at[0], partner).start()

        def ints_on(p):
            @pl.when(has_end)
            def _():
                for d in range(1, ng):
                    ints_arrive(group_of(d) + c, p)
                    ints_piece(ints_end, group_of(d) + c, p, ssem_bc.at[d], partner).start()

        def ints_last():
            for p in range(nb):
                for d in range(ng):
                    ints_arrive(group_of(d) + (1 - c), p)
            for copy in end_rows():
                copy.wait_recv()
            copy = pltpu.make_async_copy(keep_land, keep_end, lsem.at[5])
            copy.start()
            copy.wait()

        def compute_end(i):
            for q in (2 * i, 2 * i + 1):
                for zz in range(1, nz - 1):
                    arrive(zz * 2 + (1 - y), q)

                @pl.when(jnp.logical_not(crosses_early(q)))
                def _():
                    arrive(1 - y, q)
                    arrive((nz - 1) * 2 + (1 - y), q)

            mask_rows(i)

            @pl.when(has_end)
            def _():
                @pl.when(i == 0)
                def _():
                    ints_last()

                def store_end(t, value):
                    tiles_end[t] = value

                update(i, ints_end, keep_end, vir_end, store_end, lambda q: back_piece(q).start())

        def compute_own(i):
            def store_own(t, value):
                tiles[o, t] = value

            update(i, ints_own, keep, vir, store_own, share_out)

            @pl.when(i >= 2)
            def _():
                hand_on(2 * i - 4)
                hand_on(2 * i - 3)

        b_in = {1: (0, 1), 3: (2, 3), 5: (4, 5, 6), 7: (7,)}
        b_on = {3: (0, 1), 5: (2, 3), 6: (4, 5), 7: (6,), 9: (7,)}
        lag = 2 * (nz - 3) + 2

        def near_part(n):
            within(n + ahead, send_side)
            for j in range(1, nz - 2):
                within(n - (j - 1), functools.partial(from_inner, j))

        def parts_at(s, events, body):
            for at, parts in events.items():
                @pl.when(s == at)
                def _():
                    for p in parts:
                        body(p)

        def before(s):
            parts_at(s, b_in, from_outward)

            @pl.when(s == 2)
            def _():
                load_ints.wait()
                load_amps.wait()
                table()

        def far_part(e):
            for j in range(1, nz - 1):
                within(e - 2 * (j - 1), functools.partial(from_end, j))

        def loop(low, high, body):
            def one(i, carry):
                body(i)
                return carry

            lax.fori_loop(low, high, one, 0)

        if nz == 4:
            def opening(s):
                near_part(s)
                before(s)
                parts_at(s, b_on, ints_on)

            def early_step(e):
                near_part(lead + e - e // 4)
                before(lead + e)
                far_part(e)
                parts_at(lead + e, b_on, ints_on)

            def step(e):
                @pl.when(e % 4 != 3)
                def _():
                    near_part(lead + e - e // 4)

                far_part(e)

            def pair(k):
                step(2 * k + lag + 1)
                compute_end(k)
                step(2 * k + lag + 2)
                compute_own(k)

            def dense(k):
                step(k + nc + lag - 3)
                compute_end(k)
                compute_own(k)

            def closing(k):
                step(2 * k + lag - 1)
                compute_end(k)
                step(2 * k + lag)
                compute_own(k)

            loop(0, lead, opening)
            loop(0, 3, early_step)
            loop(3, 4, lambda e: (before(lead + e), far_part(e), parts_at(lead + e, b_on, ints_on)))
            loop(4, lag + 1, step)
            loop(0, nc - 4, pair)
            loop(nc - 4, nc - 2, dense)
            loop(nc - 2, nc, closing)
        else:
            def step(s):
                near_part(s)
                before(s)
                e = s - lead
                far_part(e)
                parts_at(s, b_on, ints_on)

                @pl.when((e > lag) & ((e - lag) % 2 == 1) & (e < lag + 2 * nc))
                def _():
                    k = (e - lag - 1) // 2
                    compute_end(k)
                    compute_own(k)

            loop(0, lead + np_ + lag, step)

        for i in range(np_ - 4, np_):
            hand_on(i)

    def last(i, carry):
        for d in range(ng):
            tile_piece(group_of(d) + (1 - c), i, ssem_c.at[d], partner).wait_recv()
        return carry

    lax.fori_loop(0, np_, last, 0)

    def source(s, carry):
        def slot(k, position):
            t = nxt[s, position]
            tile = tiles[s, jnp.minimum(t, td - 1)]
            out[s * cap + k] = jnp.where(t < td, tile, jnp.zeros_like(tile))
            return jnp.minimum(t + 1, td)

        lax.fori_loop(0, cap, slot, jnp.int32(0))
        return carry

    lax.fori_loop(0, no, source, 0)

    def sent(whole, send_sem, recv_sem):
        pltpu.make_async_remote_copy(
            src_ref=whole, dst_ref=whole, send_sem=send_sem, recv_sem=recv_sem,
            device_id=partner, device_id_type=MESH).wait_send()

    def sent_rows(count, direction, slot):
        if count:
            sent(gath.at[0, pl.ds(0, count)], ssem_g.at[direction, slot], rsem_g.at[0, 0])

    @pl.when(is_end)
    def _():
        sent_rows(early, 2, v)
        sent_rows(rows, 0, v)
        sent_rows(early, 0, mate)
        sent(ints_end.at[pl.ds(0, share)], ssem_b.at[0], rsem_b.at[0, 0])
        for copy in end_rows():
            copy.wait_send()

    @pl.when(inner)
    def _():
        sent_rows(rows, 2, v)
        for zz in range(nz):
            is_far = zz in (0, nz - 1)
            for direction, ok, along in ((0, go_up, zz <= z), (1, go_down, zz >= z)):
                @pl.when(ok & along)
                def _():
                    sent_rows(rows, direction, zz * 2 + y)
                    if is_far:
                        sent_rows(early, direction, zz * 2 + (1 - y))

            @pl.when(zz != z)
            def _():
                sent_rows(rows - early if is_far else rows, 2, zz * 2 + y)

        @pl.when(has_end)
        def _():
            for d in range(ng):
                whole = ints_end.at[pl.ds(0, share)]
                sent(whole, ssem_bc.at[d], rsem_b.at[0, 0])
                if d:
                    sent(whole, ssem_bx.at[d], rsem_b.at[0, 0])
            sent(tiles_end, ssem_r.at[0], rsem_t.at[0, 0])

    for d in range(ng):
        sent(tiles.at[d], ssem_c.at[d], rsem_t.at[0, 0])
        if d:
            sent(tiles.at[d], ssem_t.at[d], rsem_t.at[0, 0])
    for d in range(1, no):
        for copy in small(d, o):
            copy.wait_send()


def shards(no, nv, amps, ints, amp_mask, keep_mask, owners, occ_energy, vir_energy, mix):
    td, k_tiles = amp_mask.shape
    rows, kw = amps.shape
    tr = rows // td
    cols = ints.shape[1]
    k_tile = ints.shape[0] // k_tiles
    cap = max(2, 2 * td // no)
    chunk_tiles = max(1, min(td, 128 // tr))
    nc = td // chunk_tiles
    pieces = 2 * nc
    ahead, lead, nb, late = 4, 6, 8, 3 * pieces // 4
    cfg = (no, nv, td, tr, chunk_tiles, k_tile, ahead, lead, nb, late)
    smem = pl.BlockSpec(memory_space=pltpu.SMEM)
    vmem = pl.BlockSpec(memory_space=pltpu.VMEM)
    hbm = pl.BlockSpec(memory_space=pl.ANY)
    ng = no // 2
    own = owners.reshape(1, td)
    keep = keep_mask.reshape(1, td)
    dma = pltpu.SemaphoreType.DMA
    return pl.pallas_call(
        functools.partial(ladder_kernel, cfg),
        out_shape=jax.ShapeDtypeStruct((no * cap, tr, cols), jnp.bfloat16),
        in_specs=[hbm, hbm, smem, smem, smem, vmem, vmem, vmem, vmem, vmem],
        out_specs=vmem,
        scratch_shapes=[
            pltpu.VMEM((nv, rows, kw), jnp.bfloat16),
            pltpu.VMEM(ints.shape, jnp.bfloat16),
            pltpu.VMEM(ints.shape, jnp.bfloat16),
            pltpu.VMEM((nv, chunk_tiles * tr, kw), jnp.bfloat16),
            pltpu.VMEM((rows, 128), jnp.float32),
            pltpu.VMEM((no, td, tr, cols), jnp.bfloat16),
            pltpu.VMEM((td, tr, cols), jnp.bfloat16),
            pltpu.VMEM((no, tr, tr), jnp.bfloat16),
            pltpu.VMEM((no, 1, td), jnp.int32),
            pltpu.SMEM((no, 1, td), jnp.int32),
            pltpu.SMEM((no, td + 1), jnp.int32),
            pltpu.VMEM((1, cols), jnp.float32),
            pltpu.VMEM((1, td), jnp.int32),
            pltpu.SMEM((1, td), jnp.int32),
            dma((6,)),
            dma((nv, pieces)),
            dma((3, nv)),
            dma((no, nb)),
            dma((1,)),
            dma((ng,)),
            dma((ng,)),
            dma((no, pieces)),
            dma((ng,)),
            dma((ng,)),
            dma((1,)),
            dma((2, no)),
            dma((2, no)),
            dma((2,)),
            dma((2,)),
        ],
        compiler_params=pltpu.CompilerParams(
            collective_id=0, has_side_effects=True, vmem_limit_bytes=60 * 1024 * 1024
        ),
    )(
        amps, ints, amp_mask.T, keep, own, own,
        occ_energy.reshape(rows // 128, 128),
        vir_energy.reshape(1, cols), mix, keep,
    )


def solution(mesh):
    in_specs = (
        P("occ", "vir"),
        P(None, "vir"),
        P("occ", None),
        P("occ", "vir"),
        P("occ", None),
        P("occ"),
        P("vir"),
        P("occ", None, None),
    )
    body = functools.partial(shards, mesh.shape["occ"], mesh.shape["vir"])
    return jax.shard_map(
        body, mesh=mesh, in_specs=in_specs, out_specs=P("occ", None, "vir"), check_vma=False
    )
```

```python
import functools

import jax
import jax.numpy as jnp
from jax import lax
from jax.experimental import pallas as pl
from jax.experimental.pallas import tpu as pltpu
from jax.sharding import PartitionSpec as P

MESH = pl.DeviceIdType.MESH


def ladder_kernel(
    cfg, amps, ints, amp_mask_in, keep_in, own_in, occ_in, vir_in, mix, tiles, order,
    amp_mask, keep, own_s, occ, vir, gath, ints_own, ints_end, masked, occ_col, tiles_end, mix_all, own_all, own_tab, nxt,
    vir_end, keep_land, keep_end,
    lsem, rsem_n, rsem_e, ssem_g, rsem_b, ssem_b, ssem_bx, ssem_bc, rsem_t, ssem_c, ssem_t, ssem_r,
    rsem_o, ssem_o, rsem_s, ssem_s,
):
    no, nv, td, tr, chunk_tiles, k_tile, lead, nb, late = cfg
    ng, nz = no // 2, nv // 2
    rows, kw = amps.shape
    depth, cols = ints.shape
    cr = chunk_tiles * tr
    nc = rows // cr
    pt = chunk_tiles // 2
    pr = pt * tr
    np_ = rows // pr
    share = depth // no
    part = share // nb
    o, v = lax.axis_index("occ"), lax.axis_index("vir")
    g, c = o // 2, o % 2
    z, y = v // 2, v % 2
    mate = z * 2 + (1 - y)
    is_end = (z == 0) | (z == nz - 1)
    inner = jnp.logical_not(is_end)
    has_end = (z == 1) | (z == nz - 2)
    go_up = (z >= 1) & (z < nz - 2)
    go_down = (z > 1) & (z <= nz - 2)
    partner = {"occ": g * 2 + (1 - c), "vir": v}
    side = {"occ": o, "vir": mate}
    above = {"occ": o, "vir": (z + 1) * 2 + y}
    below = {"occ": o, "vir": (z - 1) * 2 + y}
    inward = {"occ": o, "vir": jnp.where(z == 0, 1, nz - 2) * 2 + y}
    outward = {"occ": o, "vir": jnp.where(z == 1, 0, nz - 1) * 2 + y}

    barrier = pltpu.get_barrier_semaphore()

    def greet(device):
        pl.semaphore_signal(barrier, inc=1, device_id=device, device_id_type=MESH)

    for d in range(1, no):
        greet({"occ": (o + d) % no, "vir": v})
    greet(side)

    @pl.when(z < nz - 1)
    def _():
        greet(above)

    @pl.when(z > 0)
    def _():
        greet(below)

    load_own = pltpu.make_async_copy(own_in, own_all.at[o], lsem.at[0])
    load_mix = pltpu.make_async_copy(mix.at[0], mix_all.at[o], lsem.at[1])
    load_ints = pltpu.make_async_copy(ints, ints_own, lsem.at[2])
    load_amps = pltpu.make_async_copy(amps, gath.at[v], lsem.at[3])
    loads = [
        pltpu.make_async_copy(src, dst, lsem.at[7 + n])
        for n, (src, dst) in enumerate(
            ((amp_mask_in, amp_mask), (keep_in, keep), (own_in, own_s), (occ_in, occ), (vir_in, vir)))
    ]
    load_own.start()
    load_mix.start()

    @pl.when(inner)
    def _():
        for copy in loads:
            copy.start()
        load_amps.start()
        load_ints.start()

    both = jnp.where(z < nz - 1, 1, 0) + jnp.where(z > 0, 1, 0)
    pl.semaphore_wait(barrier, no + both)

    def crosses_early(i):
        return (i < late) | (i >= late + np_ // 2) | (i % 2 == 1)

    early = sum(1 for i in range(np_) if i < late or i >= late + np_ // 2 or i % 2 == 1) * pr

    def piece(src, slot, far, i, send_sem, device):
        window = pl.ds(pl.multiple_of(i * pr, pr), pr)
        return pltpu.make_async_remote_copy(
            src_ref=src.at[window], dst_ref=gath.at[slot, window], send_sem=send_sem,
            recv_sem=rsem_e.at[far, i], device_id=device, device_id_type=MESH,
        )

    def chunk(src, slot, i, send_sem, device):
        window = pl.ds(pl.multiple_of(i * cr, cr), cr)
        return pltpu.make_async_remote_copy(
            src_ref=src.at[window], dst_ref=gath.at[slot, window], send_sem=send_sem,
            recv_sem=rsem_n.at[slot - 2, i], device_id=device, device_id_type=MESH,
        )

    def arrive(slot, far, i):
        piece(gath.at[slot], slot, far, i, ssem_g.at[2, 0], side).wait_recv()

    def arrive_chunk(slot, i):
        chunk(gath.at[slot], slot, i, ssem_g.at[2, 0], side).wait_recv()

    def small(d, o2):
        peer = {"occ": (o + d) % no, "vir": v}
        return [
            pltpu.make_async_remote_copy(
                src_ref=own_in, dst_ref=own_all.at[o2], send_sem=ssem_o.at[0, d],
                recv_sem=rsem_o.at[0, o2], device_id=peer, device_id_type=MESH),
            pltpu.make_async_remote_copy(
                src_ref=mix.at[0], dst_ref=mix_all.at[o2], send_sem=ssem_o.at[1, d],
                recv_sem=rsem_o.at[1, o2], device_id=peer, device_id_type=MESH),
        ]

    def end_rows():
        return [
            pltpu.make_async_remote_copy(
                src_ref=vir_in, dst_ref=vir_end, send_sem=ssem_s.at[0], recv_sem=rsem_s.at[0],
                device_id=inward, device_id_type=MESH),
            pltpu.make_async_remote_copy(
                src_ref=keep_in, dst_ref=keep_land, send_sem=ssem_s.at[1], recv_sem=rsem_s.at[1],
                device_id=inward, device_id_type=MESH),
        ]

    def table():
        for d in range(1, no):
            for copy in small(d, (o + d) % no):
                copy.wait_recv()
        load_own.wait()
        load_mix.wait()
        copy = pltpu.make_async_copy(own_all, own_tab, lsem.at[4])
        copy.start()
        copy.wait()

        def scan_source(s, carry):
            nxt[s, td] = td

            def back(n, following):
                t = td - 1 - n
                following = jnp.where(own_tab[s, 0, t] == o, t, following)
                nxt[s, t] = following
                return following

            lax.fori_loop(0, td, back, jnp.int32(td))
            return carry

        lax.fori_loop(0, no, scan_source, 0)
        copy = pltpu.make_async_copy(nxt, order, lsem.at[6])
        copy.start()
        copy.wait()

    def group_of(d):
        return ((g + d) % ng) * 2

    def tile_piece(o2, i, send_sem, device):
        window = pl.ds(i * pt, pt)
        return pltpu.make_async_remote_copy(
            src_ref=tiles.at[o2, window], dst_ref=tiles.at[o2, window], send_sem=send_sem,
            recv_sem=rsem_t.at[o2, i], device_id=device, device_id_type=MESH,
        )

    def back_piece(i):
        window = pl.ds(i * pt, pt)
        return pltpu.make_async_remote_copy(
            src_ref=tiles_end.at[window], dst_ref=tiles.at[o, window], send_sem=ssem_r.at[0],
            recv_sem=rsem_t.at[o, i], device_id=outward, device_id_type=MESH,
        )

    def share_out(i):
        for d in range(1, ng):
            tile_piece(o, i, ssem_t.at[d], {"occ": group_of(d) + c, "vir": v}).start()
        tile_piece(o, i, ssem_c.at[0], partner).start()

    def hand_on(i):
        for d in range(1, ng):
            o2 = group_of(d) + c
            tile_piece(o2, i, ssem_c.at[d], partner).wait_recv()
            tile_piece(o2, i, ssem_c.at[d], partner).start()

    def block(q, p):
        return pl.ds(pl.multiple_of(q * share + p * part, part), part)

    def ints_piece(src, q, p, send_sem, device):
        return pltpu.make_async_remote_copy(
            src_ref=src.at[block(q, p)], dst_ref=ints_end.at[block(q, p)], send_sem=send_sem,
            recv_sem=rsem_b.at[q, p], device_id=device, device_id_type=MESH,
        )

    def ints_arrive(q, p):
        ints_piece(ints_end, q, p, ssem_b.at[0], partner).wait_recv()

    @pl.when(is_end)
    def _():
        own_far = z // (nz - 1) * 2 + y
        mate_far = z // (nz - 1) * 2 + (1 - y)
        for copy in end_rows():
            copy.start()

        def cross(i, carry):
            @pl.when(crosses_early(i))
            def _():
                piece(amps, v, own_far, i, ssem_g.at[2, v], side).start()

            return carry

        lax.fori_loop(0, np_, cross, 0)

        def send_ints(p):
            ints_piece(ints, o, p, ssem_b.at[0], inward).start()

        def send_amps(i):
            piece(amps, v, own_far, i, ssem_g.at[0, v], inward).start()

            @pl.when(crosses_early(i))
            def _():
                arrive(mate, mate_far, i)
                piece(gath.at[mate], mate, mate_far, i, ssem_g.at[0, mate], inward).start()

        for p in range(nb - 1):
            send_ints(p)
        for d in range(1, no):
            for copy in small(d, o):
                copy.start()
        send_amps(0)
        send_ints(nb - 1)

        def rest(i, carry):
            send_amps(i)
            return carry

        lax.fori_loop(1, np_, rest, 0)
        table()

        def pass_on(i, carry):
            tile_piece(o, i, ssem_c.at[0], partner).wait_recv()
            share_out(i)

            @pl.when(i >= 3)
            def _():
                hand_on(i - 3)

            return carry

        lax.fori_loop(0, np_, pass_on, 0)
        for i in range(np_ - 3, np_):
            hand_on(i)

    def mask_rows(i):
        first = pl.multiple_of(i * cr, cr)
        for slot in range(nv):
            rows_in = gath[slot, pl.ds(first, cr), :]
            column = slot * kw + lax.broadcasted_iota(jnp.int32, (1, kw), 1)
            low, high = slot * kw // k_tile, ((slot + 1) * kw - 1) // k_tile
            for n in range(chunk_tiles):
                t = i * chunk_tiles + n
                flag = jnp.full((1, kw), amp_mask[low, t].astype(jnp.float32))
                for s in range(low + 1, high + 1):
                    flag = jnp.where(column >= s * k_tile, amp_mask[s, t].astype(jnp.float32), flag)
                flag = jnp.broadcast_to(flag, (tr, kw)).astype(jnp.bfloat16)
                masked[i % 2, slot, n * tr:(n + 1) * tr, :] = rows_in[n * tr:(n + 1) * tr] * flag

    def ladder_of(i, right):
        if kw % 128 == 0:
            left = jnp.concatenate([masked[i % 2, slot] for slot in range(nv)], axis=1)
            return jnp.dot(left, right[...], preferred_element_type=jnp.float32)
        total = jnp.zeros((cr, cols), jnp.float32)
        for slot in range(nv):
            total += jnp.dot(
                masked[i % 2, slot], right[slot * kw:(slot + 1) * kw, :], preferred_element_type=jnp.float32)
        return total

    def update(i, right, keep_row, vir_row, store, send):
        ladder = ladder_of(i, right).astype(jnp.bfloat16)
        for n in range(chunk_tiles):
            t = i * chunk_tiles + n
            kept = ladder[n * tr:(n + 1) * tr] * keep_row[0, t].astype(jnp.float32).astype(jnp.bfloat16)
            mixed = jnp.dot(mix_all[own_s[0, t]], kept, preferred_element_type=jnp.float32)
            energy = occ_col[pl.ds(pl.multiple_of(t * tr, tr), tr), :]
            denominator = vir_row[...] - jnp.concatenate([energy] * (cols // 128), axis=1)
            store(t, (mixed / denominator).astype(jnp.bfloat16))
            if n % pt == pt - 1:
                send(2 * i + n // pt)

    @pl.when(inner)
    def _():
        def send_own(i):
            @pl.when(go_up)
            def _():
                chunk(amps, v, i, ssem_g.at[0, v], above).start()

            @pl.when(go_down)
            def _():
                chunk(amps, v, i, ssem_g.at[1, v], below).start()

        def send_side(i):
            chunk(amps, v, i, ssem_g.at[2, v], side).start()

        def all_own(i, carry):
            send_own(i)
            send_side(i)
            return carry

        lax.fori_loop(0, nc, all_own, 0)
        for d in range(1, no):
            for copy in small(d, o):
                copy.start()

        for copy in loads:
            copy.wait()
        lanes = occ.shape[1]
        for r in range(occ.shape[0]):
            row = jnp.broadcast_to(occ[...].astype(jnp.float32)[r:r + 1], (128, lanes))
            occ_col[r * lanes:(r + 1) * lanes, :] = jnp.transpose(row)

        def within(i, count, body):
            @pl.when((i >= 0) & (i < count))
            def _():
                body(i)

        def relay(copy, slot, up):
            ok, sem, device = (go_up, 0, above) if up else (go_down, 1, below)

            @pl.when(ok)
            def _():
                copy(ssem_g.at[sem, slot], device).start()

        def from_inner(j, i):
            for near, up in ((z - j, True), (z + j, False)):
                @pl.when((near >= 1) & (near <= nz - 2))
                def _():
                    slot = near * 2 + y
                    arrive_chunk(slot, i)
                    relay(functools.partial(chunk, gath.at[slot], slot, i), slot, up)
                    chunk(gath.at[slot], slot, i, ssem_g.at[2, slot], side).start()

        def from_end(j, i):
            for near, end, first, up in ((z - j, 0, 0, True), (z + j, nz - 1, 2, False)):
                @pl.when(near == end)
                def _():
                    slot = end * 2 + y
                    other = end * 2 + (1 - y)
                    arrive(slot, first + y, i)
                    relay(functools.partial(piece, gath.at[slot], slot, first + y, i), slot, up)

                    @pl.when(crosses_early(i))
                    def _():
                        arrive(other, first + (1 - y), i)
                        relay(functools.partial(piece, gath.at[other], other, first + (1 - y), i), other, up)

                    @pl.when(jnp.logical_not(crosses_early(i)))
                    def _():
                        piece(gath.at[slot], slot, first + y, i, ssem_g.at[2, slot], side).start()

        def from_outward(p):
            @pl.when(has_end)
            def _():
                ints_arrive(o, p)
                for d in range(1, ng):
                    ints_piece(ints_end, o, p, ssem_bx.at[d], {"occ": group_of(d) + c, "vir": v}).start()
                ints_piece(ints_end, o, p, ssem_bc.at[0], partner).start()

        def ints_on(p):
            @pl.when(has_end)
            def _():
                for d in range(1, ng):
                    ints_arrive(group_of(d) + c, p)
                    ints_piece(ints_end, group_of(d) + c, p, ssem_bc.at[d], partner).start()

        def ints_last():
            for p in range(nb):
                for d in range(ng):
                    ints_arrive(group_of(d) + (1 - c), p)
            for copy in end_rows():
                copy.wait_recv()
            copy = pltpu.make_async_copy(keep_land, keep_end, lsem.at[5])
            copy.start()
            copy.wait()

        def compute_end(i):
            for zz in range(1, nz - 1):
                arrive_chunk(zz * 2 + (1 - y), i)
            for q in (2 * i, 2 * i + 1):
                @pl.when(jnp.logical_not(crosses_early(q)))
                def _():
                    arrive(1 - y, 1 - y, q)
                    arrive((nz - 1) * 2 + (1 - y), 2 + (1 - y), q)

            mask_rows(i)

            @pl.when(has_end)
            def _():
                @pl.when(i == 0)
                def _():
                    ints_last()

                def store_end(t, value):
                    tiles_end[t] = value

                update(i, ints_end, keep_end, vir_end, store_end, lambda q: back_piece(q).start())

        def compute_own(i):
            def store_own(t, value):
                tiles[o, t] = value

            update(i, ints_own, keep, vir, store_own, share_out)

            @pl.when(i >= 2)
            def _():
                hand_on(2 * i - 4)
                hand_on(2 * i - 3)

        b_in = {1: (0, 1), 3: (2, 3), 5: (4, 5, 6), 7: (7,)}
        b_on = {3: (0, 1), 5: (2, 3), 6: (4, 5), 7: (6,), 9: (7,)}
        lag = 2 * (nz - 3) + 2
        assert nz >= 4 and np_ == 2 * nc

        def near_part(n):
            for j in range(1, nz - 2):
                within(n - (j - 1), nc, functools.partial(from_inner, j))

        def parts_at(s, events, body):
            for at, parts in events.items():
                @pl.when(s == at)
                def _():
                    for p in parts:
                        body(p)

        def before(s):
            parts_at(s, b_in, from_outward)

            @pl.when(s == 2)
            def _():
                load_ints.wait()
                load_amps.wait()
                table()

        def far_part(e):
            for j in range(1, nz - 1):
                within(e - 2 * (j - 1), np_, functools.partial(from_end, j))

        def loop(low, high, body):
            def one(i, carry):
                body(i)
                return carry

            lax.fori_loop(low, high, one, 0)

        if nz == 4:
            def opening(s):
                near_part(s)
                before(s)
                parts_at(s, b_on, ints_on)

            def early_step(e):
                near_part(lead + e)
                before(lead + e)
                far_part(e)
                parts_at(lead + e, b_on, ints_on)


            def pair(k):
                far_part(2 * k + 4)
                compute_end(k)
                far_part(2 * k + 5)
                compute_own(k)

            loop(0, lead, opening)
            loop(0, 4, early_step)
            loop(0, nc - 2, pair)
            compute_end(nc - 2)
            far_part(np_)
            far_part(np_ + 1)
            compute_end(nc - 1)
            compute_own(nc - 2)
            compute_own(nc - 1)
        else:
            def step(s):
                near_part(s)
                before(s)
                e = s - lead
                far_part(e)
                parts_at(s, b_on, ints_on)

                @pl.when((e > lag) & ((e - lag) % 2 == 1) & (e < lag + 2 * nc))
                def _():
                    k = (e - lag - 1) // 2
                    compute_end(k)
                    compute_own(k)

            loop(0, lead + np_ + lag, step)

        for i in range(np_ - 4, np_):
            hand_on(i)

    def last(i, carry):
        for d in range(ng):
            tile_piece(group_of(d) + (1 - c), i, ssem_c.at[d], partner).wait_recv()
        return carry

    lax.fori_loop(0, np_, last, 0)

    def sent(whole, send_sem, recv_sem):
        pltpu.make_async_remote_copy(
            src_ref=whole, dst_ref=whole, send_sem=send_sem, recv_sem=recv_sem,
            device_id=partner, device_id_type=MESH).wait_send()

    def sent_rows(count, direction, slot):
        if count:
            sent(gath.at[0, pl.ds(0, count)], ssem_g.at[direction, slot], rsem_e.at[0, 0])

    @pl.when(is_end)
    def _():
        sent_rows(early, 2, v)
        sent_rows(rows, 0, v)
        sent_rows(early, 0, mate)
        sent(ints_end.at[pl.ds(0, share)], ssem_b.at[0], rsem_b.at[0, 0])
        for copy in end_rows():
            copy.wait_send()

    @pl.when(inner)
    def _():
        sent_rows(rows, 2, v)
        for zz in range(nz):
            is_far = zz in (0, nz - 1)
            for direction, ok, along in ((0, go_up, zz <= z), (1, go_down, zz >= z)):
                @pl.when(ok & along)
                def _():
                    sent_rows(rows, direction, zz * 2 + y)
                    if is_far:
                        sent_rows(early, direction, zz * 2 + (1 - y))

            @pl.when(zz != z)
            def _():
                sent_rows(rows - early if is_far else rows, 2, zz * 2 + y)

        @pl.when(has_end)
        def _():
            for d in range(ng):
                whole = ints_end.at[pl.ds(0, share)]
                sent(whole, ssem_bc.at[d], rsem_b.at[0, 0])
                if d:
                    sent(whole, ssem_bx.at[d], rsem_b.at[0, 0])
            sent(tiles_end, ssem_r.at[0], rsem_t.at[0, 0])

    for d in range(ng):
        sent(tiles.at[d], ssem_c.at[d], rsem_t.at[0, 0])
        if d:
            sent(tiles.at[d], ssem_t.at[d], rsem_t.at[0, 0])
    for d in range(1, no):
        for copy in small(d, o):
            copy.wait_send()


def place_kernel(cap, order, tiles, out, blank, sem):
    no, td = tiles.shape[:2]
    blank[...] = jnp.zeros_like(blank)

    def source(s, carry):
        def slot(k, position):
            t = order[s, position]

            @pl.when(t < td)
            def _():
                pltpu.make_async_copy(tiles.at[s, t], out.at[s * cap + k], sem).start()

            @pl.when(t >= td)
            def _():
                pltpu.make_async_copy(blank, out.at[s * cap + k], sem).start()

            return jnp.minimum(t + 1, td)

        lax.fori_loop(0, cap, slot, jnp.int32(0))
        return carry

    lax.fori_loop(0, no, source, 0)
    pltpu.make_async_copy(out, out, sem).wait()


def shards(no, nv, amps, ints, amp_mask, keep_mask, owners, occ_energy, vir_energy, mix):
    td, k_tiles = amp_mask.shape
    rows, kw = amps.shape
    tr = rows // td
    cols = ints.shape[1]
    k_tile = ints.shape[0] // k_tiles
    cap = max(2, 2 * td // no)
    chunk_tiles = max(1, min(td, 128 // tr))
    nc = td // chunk_tiles
    pieces = 2 * nc
    lead, nb, late = 6, 8, 3 * pieces // 8
    cfg = (no, nv, td, tr, chunk_tiles, k_tile, lead, nb, late)
    smem = pl.BlockSpec(memory_space=pltpu.SMEM)
    vmem = pl.BlockSpec(memory_space=pltpu.VMEM)
    hbm = pl.BlockSpec(memory_space=pl.ANY)
    ng = no // 2
    own = owners.reshape(1, td)
    keep = keep_mask.reshape(1, td)
    dma = pltpu.SemaphoreType.DMA
    room = (63 << 20) - no * td * tr * cols * 2
    tiles, order = pl.pallas_call(
        functools.partial(ladder_kernel, cfg),
        out_shape=(
            pltpu.VMEM((no, td, tr, cols), jnp.bfloat16),
            pltpu.VMEM((no, td + 1), jnp.int32),
        ),
        in_specs=[hbm] * 8,
        out_specs=(vmem, hbm),
        scratch_shapes=[
            pltpu.SMEM((k_tiles, td), jnp.int32),
            pltpu.SMEM((1, td), jnp.int32),
            pltpu.SMEM((1, td), jnp.int32),
            pltpu.VMEM((rows // 128, 128), jnp.bfloat16),
            pltpu.VMEM((1, cols), jnp.float32),
            pltpu.VMEM((nv, rows, kw), jnp.bfloat16),
            pltpu.VMEM(ints.shape, jnp.bfloat16),
            pltpu.VMEM(ints.shape, jnp.bfloat16),
            pltpu.VMEM((2, nv, chunk_tiles * tr, kw), jnp.bfloat16),
            pltpu.VMEM((rows, 128), jnp.float32),
            pltpu.VMEM((td, tr, cols), jnp.bfloat16),
            pltpu.VMEM((no, tr, tr), jnp.bfloat16),
            pltpu.VMEM((no, 1, td), jnp.int32),
            pltpu.SMEM((no, 1, td), jnp.int32),
            pltpu.SMEM((no, td + 1), jnp.int32),
            pltpu.VMEM((1, cols), jnp.float32),
            pltpu.VMEM((1, td), jnp.int32),
            pltpu.SMEM((1, td), jnp.int32),
            dma((12,)),
            dma((nv - 4, nc)),
            dma((4, pieces)),
            dma((3, nv)),
            dma((no, nb)),
            dma((1,)),
            dma((ng,)),
            dma((ng,)),
            dma((no, pieces)),
            dma((ng,)),
            dma((ng,)),
            dma((1,)),
            dma((2, no)),
            dma((2, no)),
            dma((2,)),
            dma((2,)),
        ],
        compiler_params=pltpu.CompilerParams(
            collective_id=0, has_side_effects=True, vmem_limit_bytes=room
        ),
    )(
        amps, ints, amp_mask.T, keep, own, occ_energy.reshape(rows // 128, 128),
        vir_energy.reshape(1, cols), mix,
    )
    return pl.pallas_call(
        functools.partial(place_kernel, cap),
        out_shape=jax.ShapeDtypeStruct((no * cap, tr, cols), jnp.bfloat16),
        in_specs=[smem, vmem],
        out_specs=hbm,
        scratch_shapes=[pltpu.VMEM((tr, cols), jnp.bfloat16), dma],
        compiler_params=pltpu.CompilerParams(vmem_limit_bytes=24 * 1024 * 1024),
    )(order, tiles)


def solution(mesh):
    in_specs = (
        P("occ", "vir"),
        P(None, "vir"),
        P("occ", None),
        P("occ", "vir"),
        P("occ", None),
        P("occ"),
        P("vir"),
        P("occ", None, None),
    )
    body = functools.partial(shards, mesh.shape["occ"], mesh.shape["vir"])
    return jax.shard_map(
        body, mesh=mesh, in_specs=in_specs, out_specs=P("occ", None, "vir"), check_vma=False
    )
```

```python
import functools
import operator

import jax
import jax.numpy as jnp
from jax import lax
from jax.experimental import pallas as pl
from jax.experimental.pallas import tpu as pltpu
from jax.sharding import PartitionSpec as P

MESH = pl.DeviceIdType.MESH


def ladder_kernel(
    cfg, amps, ints, amp_mask_in, keep_in, own_in, occ_in, vir_in, mix, tiles, order,
    amp_mask, keep, own_s, occ, vir, gath, ints_own, ints_end, masked, occ_col, tiles_end, mix_all, own_all, own_tab, nxt,
    vir_end, keep_land, keep_end,
    lsem, rsem_n, rsem_e, ssem_g, rsem_b, ssem_b, ssem_bx, ssem_bc, rsem_t, ssem_c, ssem_t, ssem_r,
    rsem_o, ssem_o, rsem_s, ssem_s,
):
    no, nv, td, tr, chunk_tiles, k_tile, lead, nb, late = cfg
    ng, nz = no // 2, nv // 2
    rows, kw = amps.shape
    depth, cols = ints.shape
    cr = chunk_tiles * tr
    nc = rows // cr
    pt = chunk_tiles // 2
    pr = pt * tr
    np_ = rows // pr
    share = depth // no
    part = share // nb
    o, v = lax.axis_index("occ"), lax.axis_index("vir")
    g, c = o // 2, o % 2
    z, y = v // 2, v % 2
    mate = z * 2 + (1 - y)
    is_end = (z == 0) | (z == nz - 1)
    inner = jnp.logical_not(is_end)
    has_end = (z == 1) | (z == nz - 2)
    go_up = (z >= 1) & (z < nz - 2)
    go_down = (z > 1) & (z <= nz - 2)
    partner = {"occ": g * 2 + (1 - c), "vir": v}
    side = {"occ": o, "vir": mate}
    above = {"occ": o, "vir": (z + 1) * 2 + y}
    below = {"occ": o, "vir": (z - 1) * 2 + y}
    inward = {"occ": o, "vir": jnp.where(z == 0, 1, nz - 2) * 2 + y}
    outward = {"occ": o, "vir": jnp.where(z == 1, 0, nz - 1) * 2 + y}

    barrier = pltpu.get_barrier_semaphore()

    def greet(device):
        pl.semaphore_signal(barrier, inc=1, device_id=device, device_id_type=MESH)

    for d in range(1, no):
        greet({"occ": (o + d) % no, "vir": v})
    greet(side)

    @pl.when(z < nz - 1)
    def _():
        greet(above)

    @pl.when(z > 0)
    def _():
        greet(below)

    load_own = pltpu.make_async_copy(own_in, own_all.at[o], lsem.at[0])
    load_mix = pltpu.make_async_copy(mix.at[0], mix_all.at[o], lsem.at[1])
    load_ints = pltpu.make_async_copy(ints, ints_own, lsem.at[2])
    load_amps = pltpu.make_async_copy(amps, gath.at[v], lsem.at[3])
    loads = [
        pltpu.make_async_copy(src, dst, lsem.at[7 + n])
        for n, (src, dst) in enumerate(
            ((amp_mask_in, amp_mask), (keep_in, keep), (own_in, own_s), (occ_in, occ), (vir_in, vir)))
    ]
    load_own.start()
    load_mix.start()

    @pl.when(inner)
    def _():
        for copy in loads:
            copy.start()
        load_amps.start()
        load_ints.start()

    both = jnp.where(z < nz - 1, 1, 0) + jnp.where(z > 0, 1, 0)
    pl.semaphore_wait(barrier, no + both)

    at_both, at_first = late if nz == 4 else (late[0], ())

    def among(i, pieces):
        return functools.reduce(operator.or_, [i == q for q in pieces], i < 0)

    def crosses_early(i):
        return jnp.logical_not(among(i, at_both + at_first))

    early = (np_ - len(at_both) - len(at_first)) * pr

    def piece(src, slot, far, i, send_sem, device):
        window = pl.ds(pl.multiple_of(i * pr, pr), pr)
        return pltpu.make_async_remote_copy(
            src_ref=src.at[window], dst_ref=gath.at[slot, window], send_sem=send_sem,
            recv_sem=rsem_e.at[far, i], device_id=device, device_id_type=MESH,
        )

    def chunk(src, slot, i, send_sem, device):
        window = pl.ds(pl.multiple_of(i * cr, cr), cr)
        return pltpu.make_async_remote_copy(
            src_ref=src.at[window], dst_ref=gath.at[slot, window], send_sem=send_sem,
            recv_sem=rsem_n.at[slot - 2, i], device_id=device, device_id_type=MESH,
        )

    def arrive(slot, far, i):
        piece(gath.at[slot], slot, far, i, ssem_g.at[2, 0], side).wait_recv()

    def arrive_chunk(slot, i):
        chunk(gath.at[slot], slot, i, ssem_g.at[2, 0], side).wait_recv()

    def small(d, o2):
        peer = {"occ": (o + d) % no, "vir": v}
        return [
            pltpu.make_async_remote_copy(
                src_ref=own_in, dst_ref=own_all.at[o2], send_sem=ssem_o.at[0, d],
                recv_sem=rsem_o.at[0, o2], device_id=peer, device_id_type=MESH),
            pltpu.make_async_remote_copy(
                src_ref=mix.at[0], dst_ref=mix_all.at[o2], send_sem=ssem_o.at[1, d],
                recv_sem=rsem_o.at[1, o2], device_id=peer, device_id_type=MESH),
        ]

    def end_rows():
        return [
            pltpu.make_async_remote_copy(
                src_ref=vir_in, dst_ref=vir_end, send_sem=ssem_s.at[0], recv_sem=rsem_s.at[0],
                device_id=inward, device_id_type=MESH),
            pltpu.make_async_remote_copy(
                src_ref=keep_in, dst_ref=keep_land, send_sem=ssem_s.at[1], recv_sem=rsem_s.at[1],
                device_id=inward, device_id_type=MESH),
        ]

    def table():
        for d in range(1, no):
            for copy in small(d, (o + d) % no):
                copy.wait_recv()
        load_own.wait()
        load_mix.wait()
        copy = pltpu.make_async_copy(own_all, own_tab, lsem.at[4])
        copy.start()
        copy.wait()

        def scan_source(s, carry):
            nxt[s, td] = td

            def back(n, following):
                t = td - 1 - n
                following = jnp.where(own_tab[s, 0, t] == o, t, following)
                nxt[s, t] = following
                return following

            lax.fori_loop(0, td, back, jnp.int32(td))
            return carry

        lax.fori_loop(0, no, scan_source, 0)
        copy = pltpu.make_async_copy(nxt, order, lsem.at[6])
        copy.start()
        copy.wait()

    def group_of(d):
        return ((g + d) % ng) * 2

    def tile_window(p):
        if isinstance(p, int) and p >= nc - 1:
            return pl.ds((nc - 1) * chunk_tiles + (p - nc + 1) * pt, pt)
        return pl.ds(p * chunk_tiles, chunk_tiles)

    def tile_piece(o2, i, send_sem, device):
        window = tile_window(i)
        return pltpu.make_async_remote_copy(
            src_ref=tiles.at[o2, window], dst_ref=tiles.at[o2, window], send_sem=send_sem,
            recv_sem=rsem_t.at[o2, i], device_id=device, device_id_type=MESH,
        )

    def back_piece(i):
        window = tile_window(i)
        return pltpu.make_async_remote_copy(
            src_ref=tiles_end.at[window], dst_ref=tiles.at[o, window], send_sem=ssem_r.at[0],
            recv_sem=rsem_t.at[o, i], device_id=outward, device_id_type=MESH,
        )

    def share_out(i):
        for d in range(1, ng):
            tile_piece(o, i, ssem_t.at[d], {"occ": group_of(d) + c, "vir": v}).start()
        tile_piece(o, i, ssem_c.at[0], partner).start()

    def hand_on(i):
        for d in range(1, ng):
            o2 = group_of(d) + c
            tile_piece(o2, i, ssem_c.at[d], partner).wait_recv()
            tile_piece(o2, i, ssem_c.at[d], partner).start()

    def block(q, p):
        return pl.ds(pl.multiple_of(q * share + p * part, part), part)

    def ints_piece(src, q, p, send_sem, device):
        return pltpu.make_async_remote_copy(
            src_ref=src.at[block(q, p)], dst_ref=ints_end.at[block(q, p)], send_sem=send_sem,
            recv_sem=rsem_b.at[q, p], device_id=device, device_id_type=MESH,
        )

    def ints_arrive(q, p):
        ints_piece(ints_end, q, p, ssem_b.at[0], partner).wait_recv()

    @pl.when(is_end)
    def _():
        own_far = z // (nz - 1) * 2 + y
        mate_far = z // (nz - 1) * 2 + (1 - y)
        for copy in end_rows():
            copy.start()

        def cross(i, carry):
            @pl.when(crosses_early(i))
            def _():
                piece(amps, v, own_far, i, ssem_g.at[2, v], side).start()

            return carry

        lax.fori_loop(0, np_, cross, 0)

        def send_ints(p):
            ints_piece(ints, o, p, ssem_b.at[0], inward).start()

        def send_amps(i):
            piece(amps, v, own_far, i, ssem_g.at[0, v], inward).start()

            @pl.when(crosses_early(i))
            def _():
                arrive(mate, mate_far, i)
                piece(gath.at[mate], mate, mate_far, i, ssem_g.at[0, mate], inward).start()

        for p in range(nb - 1):
            send_ints(p)
        for d in range(1, no):
            for copy in small(d, o):
                copy.start()
        send_amps(0)
        send_ints(nb - 1)

        def rest(i, carry):
            send_amps(i)
            return carry

        lax.fori_loop(1, np_, rest, 0)
        table()

        def pass_on(i):
            tile_piece(o, i, ssem_c.at[0], partner).wait_recv()
            share_out(i)

        def passing(i, carry):
            pass_on(i)

            @pl.when(i >= 2)
            def _():
                hand_on(i - 2)

            return carry

        lax.fori_loop(0, nc - 1, passing, 0)
        for i in (nc - 1, nc):
            pass_on(i)
            hand_on(i - 2)
        for i in (nc - 1, nc):
            hand_on(i)

    def mask_rows(i, tiles_in):
        first = pl.multiple_of(i * cr + tiles_in[0] * tr, tr)
        for slot in range(nv):
            rows_in = gath[slot, pl.ds(first, len(tiles_in) * tr), :]
            column = slot * kw + lax.broadcasted_iota(jnp.int32, (1, kw), 1)
            low, high = slot * kw // k_tile, ((slot + 1) * kw - 1) // k_tile
            for place, n in enumerate(tiles_in):
                t = i * chunk_tiles + n
                flag = jnp.full((1, kw), amp_mask[low, t].astype(jnp.float32))
                for s in range(low + 1, high + 1):
                    flag = jnp.where(column >= s * k_tile, amp_mask[s, t].astype(jnp.float32), flag)
                flag = jnp.broadcast_to(flag, (tr, kw)).astype(jnp.bfloat16)
                masked[i % 2, slot, n * tr:(n + 1) * tr, :] = rows_in[place * tr:(place + 1) * tr] * flag

    def ladder_of(i, tiles_in, right):
        held = pl.ds(tiles_in[0] * tr, len(tiles_in) * tr)
        if kw % 128 == 0:
            left = jnp.concatenate([masked[i % 2, slot, held, :] for slot in range(nv)], axis=1)
            return jnp.dot(left, right[...], preferred_element_type=jnp.float32)
        total = jnp.zeros((len(tiles_in) * tr, cols), jnp.float32)
        for slot in range(nv):
            total += jnp.dot(
                masked[i % 2, slot, held, :], right[slot * kw:(slot + 1) * kw, :],
                preferred_element_type=jnp.float32)
        return total

    every = range(chunk_tiles)
    halves = [range(h * pt, (h + 1) * pt) for h in range(2)]

    def update(i, tiles_in, right, keep_row, vir_row, store, send):
        ladder = ladder_of(i, tiles_in, right).astype(jnp.bfloat16)
        for place, n in enumerate(tiles_in):
            t = i * chunk_tiles + n
            kept = ladder[place * tr:(place + 1) * tr] * keep_row[0, t].astype(jnp.float32).astype(jnp.bfloat16)
            mixed = jnp.dot(mix_all[own_s[0, t]], kept, preferred_element_type=jnp.float32)
            energy = occ_col[pl.ds(pl.multiple_of(t * tr, tr), tr), :]
            denominator = vir_row[...] - jnp.concatenate([energy] * (cols // 128), axis=1)
            store(t, (mixed / denominator).astype(jnp.bfloat16))
            if isinstance(i, int) and i == nc - 1:
                if n % pt == pt - 1:
                    send(i + n // pt)
            elif n == chunk_tiles - 1:
                send(i)

    @pl.when(inner)
    def _():
        def send_own(i):
            @pl.when(go_up)
            def _():
                chunk(amps, v, i, ssem_g.at[0, v], above).start()

            @pl.when(go_down)
            def _():
                chunk(amps, v, i, ssem_g.at[1, v], below).start()

        def send_side(i):
            chunk(amps, v, i, ssem_g.at[2, v], side).start()

        def all_own(i, carry):
            send_own(i)
            send_side(i)
            return carry

        lax.fori_loop(0, nc, all_own, 0)
        for d in range(1, no):
            for copy in small(d, o):
                copy.start()

        for copy in loads:
            copy.wait()
        lanes = occ.shape[1]
        for r in range(occ.shape[0]):
            row = jnp.broadcast_to(occ[...].astype(jnp.float32)[r:r + 1], (128, lanes))
            occ_col[r * lanes:(r + 1) * lanes, :] = jnp.transpose(row)

        def within(i, count, body):
            @pl.when((i >= 0) & (i < count))
            def _():
                body(i)

        def relay(copy, slot, up):
            ok, sem, device = (go_up, 0, above) if up else (go_down, 1, below)

            @pl.when(ok)
            def _():
                copy(ssem_g.at[sem, slot], device).start()

        def from_inner(j, i):
            for near, up in ((z - j, True), (z + j, False)):
                @pl.when((near >= 1) & (near <= nz - 2))
                def _():
                    slot = near * 2 + y
                    arrive_chunk(slot, i)
                    relay(functools.partial(chunk, gath.at[slot], slot, i), slot, up)
                    chunk(gath.at[slot], slot, i, ssem_g.at[2, slot], side).start()

        def from_end(j, i):
            for near, end, first, up in ((z - j, 0, 0, True), (z + j, nz - 1, 2, False)):
                @pl.when(near == end)
                def _():
                    slot = end * 2 + y
                    other = end * 2 + (1 - y)
                    arrive(slot, first + y, i)
                    relay(functools.partial(piece, gath.at[slot], slot, first + y, i), slot, up)

                    @pl.when(crosses_early(i))
                    def _():
                        arrive(other, first + (1 - y), i)
                        relay(functools.partial(piece, gath.at[other], other, first + (1 - y), i), other, up)

                    @pl.when(jnp.logical_not(crosses_early(i)))
                    def _():
                        piece(gath.at[slot], slot, first + y, i, ssem_g.at[2, slot], side).start()

        def from_outward(p):
            @pl.when(has_end)
            def _():
                ints_arrive(o, p)
                for d in range(1, ng):
                    ints_piece(ints_end, o, p, ssem_bx.at[d], {"occ": group_of(d) + c, "vir": v}).start()
                ints_piece(ints_end, o, p, ssem_bc.at[0], partner).start()

        def ints_on(p):
            @pl.when(has_end)
            def _():
                for d in range(1, ng):
                    ints_arrive(group_of(d) + c, p)
                    ints_piece(ints_end, group_of(d) + c, p, ssem_bc.at[d], partner).start()

        def ints_last():
            for p in range(nb):
                for d in range(ng):
                    ints_arrive(group_of(d) + (1 - c), p)

        def compute_end(i, tiles_in=every):
            if tiles_in[0] == 0:
                for zz in range(1, nz - 1):
                    arrive_chunk(zz * 2 + (1 - y), i)
            for q in range(2 * i + tiles_in[0] // pt, 2 * i + tiles_in[-1] // pt + 1) if isinstance(i, int) else (2 * i, 2 * i + 1):
                if nz == 4:
                    near, far = z - 1, 2 - z

                    @pl.when(among(q, at_both))
                    def _():
                        arrive(near * 6 + 1 - y, near * 2 + 1 - y, q)

                    @pl.when(jnp.logical_not(among(q, at_both)))
                    def _():
                        arrive(far * 6 + y, far * 2 + y, q)

                    arrive(far * 6 + 1 - y, far * 2 + 1 - y, q)
                else:
                    @pl.when(jnp.logical_not(crosses_early(q)))
                    def _():
                        arrive(1 - y, 1 - y, q)
                        arrive((nz - 1) * 2 + (1 - y), 2 + (1 - y), q)

            mask_rows(i, tiles_in)

            @pl.when(has_end)
            def _():
                if not (isinstance(i, int) and i):
                    @pl.when(i == 0)
                    def _():
                        ints_last()

                def store_end(t, value):
                    tiles_end[t] = value

                update(i, tiles_in, ints_end, keep_end, vir_end, store_end, lambda q: back_piece(q).start())

        def compute_own(i):
            def store_own(t, value):
                tiles[o, t] = value

            update(i, every, ints_own, keep, vir, store_own, share_out)

            if isinstance(i, int):
                hand_on(i - 2)
            else:
                @pl.when(i >= 2)
                def _():
                    hand_on(i - 2)

        b_in = {0: (0,), 1: (1,), 2: (2,), 3: (3,), 4: (4,), 5: (5,), 6: (6,), 7: (7,)}
        b_on = {3: (0,), 4: (1,), 5: (2,), 6: (3,), 7: (4, 5), 8: (6, 7)}
        lag = 2 * (nz - 3) + 2
        assert nz >= 4 and np_ == 2 * nc

        def near_part(n):
            for j in range(1, nz - 2):
                within(n - (j - 1), nc, functools.partial(from_inner, j))

        def parts_at(s, events, body):
            for at, parts in events.items():
                @pl.when(s == at)
                def _():
                    for p in parts:
                        body(p)

        def before(s):
            parts_at(s, b_in, from_outward)

            @pl.when(s == 2)
            def _():
                load_ints.wait()
                load_amps.wait()
                table()

                @pl.when(has_end)
                def _():
                    for copy in end_rows():
                        copy.wait_recv()
                    copy = pltpu.make_async_copy(keep_land, keep_end, lsem.at[5])
                    copy.start()
                    copy.wait()

        def ends_part(e):
            near, far = z - 1, 2 - z
            across = {"occ": o, "vir": (3 - z) * 2 + y}

            def to_across(slot, far_slot, i):
                piece(gath.at[slot], slot, far_slot, i, ssem_g.at[near, slot], across).start()

            def to_side(slot, far_slot, i):
                piece(gath.at[slot], slot, far_slot, i, ssem_g.at[2, slot], side).start()

            def first(i):
                slot, other = near * 6 + y, near * 6 + 1 - y
                arrive(slot, near * 2 + y, i)
                to_across(slot, near * 2 + y, i)

                @pl.when(crosses_early(i))
                def _():
                    arrive(other, near * 2 + 1 - y, i)
                    to_across(other, near * 2 + 1 - y, i)

                @pl.when(jnp.logical_not(crosses_early(i)))
                def _():
                    to_side(slot, near * 2 + y, i)

            def second(i):
                slot, other = far * 6 + y, near * 6 + 1 - y

                @pl.when(among(i, at_both))
                def _():
                    arrive(slot, far * 2 + y, i)
                    to_side(slot, far * 2 + y, i)

                @pl.when(among(i, at_first))
                def _():
                    arrive(other, near * 2 + 1 - y, i)
                    to_across(other, near * 2 + 1 - y, i)

            within(e, np_, first)
            within(e - 2, np_, second)

        def far_part(e):
            if nz == 4:
                ends_part(e)
                return
            for j in range(1, nz - 1):
                within(e - 2 * (j - 1), np_, functools.partial(from_end, j))

        def loop(low, high, body):
            def one(i, carry):
                body(i)
                return carry

            lax.fori_loop(low, high, one, 0)

        if nz == 4:
            def opening(s):
                near_part(s)
                before(s)
                parts_at(s, b_on, ints_on)

            def early_step(e):
                near_part(lead + e)
                before(lead + e)
                far_part(e)
                parts_at(lead + e, b_on, ints_on)


            def pair(k):
                far_part(2 * k + 4)
                compute_end(k)
                far_part(2 * k + 5)
                compute_own(k)

            loop(0, lead, opening)
            loop(0, 4, early_step)
            loop(0, nc - 2, pair)
            compute_end(nc - 2)
            compute_own(nc - 2)
            for half in halves:
                compute_end(nc - 1, half)
            compute_own(nc - 1)
        else:
            def step(s):
                near_part(s)
                before(s)
                e = s - lead
                far_part(e)
                parts_at(s, b_on, ints_on)

                @pl.when((e > lag) & ((e - lag) % 2 == 1) & (e < lag + 2 * nc - 2))
                def _():
                    k = (e - lag - 1) // 2
                    compute_end(k)
                    compute_own(k)

            loop(0, lead + np_ + lag, step)
            compute_end(nc - 1)
            compute_own(nc - 1)

        for i in (nc - 2, nc - 1, nc):
            hand_on(i)

    def last(i, carry):
        for d in range(ng):
            tile_piece(group_of(d) + (1 - c), i, ssem_c.at[d], partner).wait_recv()
        return carry

    lax.fori_loop(0, nc - 1, last, 0)
    for i in (nc - 1, nc):
        last(i, 0)

    def sent(whole, send_sem, recv_sem):
        pltpu.make_async_remote_copy(
            src_ref=whole, dst_ref=whole, send_sem=send_sem, recv_sem=recv_sem,
            device_id=partner, device_id_type=MESH).wait_send()

    def sent_rows(count, direction, slot):
        if count:
            sent(gath.at[0, pl.ds(0, count)], ssem_g.at[direction, slot], rsem_e.at[0, 0])

    @pl.when(is_end)
    def _():
        sent_rows(early, 2, v)
        sent_rows(rows, 0, v)
        sent_rows(early, 0, mate)
        sent(ints_end.at[pl.ds(0, share)], ssem_b.at[0], rsem_b.at[0, 0])
        for copy in end_rows():
            copy.wait_send()

    @pl.when(inner)
    def _():
        sent_rows(rows, 2, v)
        for zz in range(nz):
            is_far = zz in (0, nz - 1)
            for direction, ok, along in ((0, go_up, zz <= z), (1, go_down, zz >= z)):
                @pl.when(ok & along)
                def _():
                    sent_rows(rows, direction, zz * 2 + y)
                    if is_far:
                        sent_rows(early + len(at_first) * pr, direction, zz * 2 + (1 - y))

            @pl.when(zz != z)
            def _():
                sent_rows(len(at_both) * pr if is_far else rows, 2, zz * 2 + y)

            if is_far and at_first:
                @pl.when(z == (1 if zz == 0 else nz - 2))
                def _():
                    sent_rows(len(at_first) * pr, 2, zz * 2 + y)

        @pl.when(has_end)
        def _():
            for d in range(ng):
                whole = ints_end.at[pl.ds(0, share)]
                sent(whole, ssem_bc.at[d], rsem_b.at[0, 0])
                if d:
                    sent(whole, ssem_bx.at[d], rsem_b.at[0, 0])
            sent(tiles_end, ssem_r.at[0], rsem_t.at[0, 0])

    for d in range(ng):
        sent(tiles.at[d], ssem_c.at[d], rsem_t.at[0, 0])
        if d:
            sent(tiles.at[d], ssem_t.at[d], rsem_t.at[0, 0])
    for d in range(1, no):
        for copy in small(d, o):
            copy.wait_send()


def place_kernel(cap, order, tiles, out, blank, sem):
    no, td = tiles.shape[:2]
    blank[...] = jnp.zeros_like(blank)

    def source(s, carry):
        def slot(k, position):
            t = order[s, position]

            @pl.when(t < td)
            def _():
                pltpu.make_async_copy(tiles.at[s, t], out.at[s * cap + k], sem).start()

            @pl.when(t >= td)
            def _():
                pltpu.make_async_copy(blank, out.at[s * cap + k], sem).start()

            return jnp.minimum(t + 1, td)

        lax.fori_loop(0, cap, slot, jnp.int32(0))
        return carry

    lax.fori_loop(0, no, source, 0)
    pltpu.make_async_copy(out, out, sem).wait()


def shards(no, nv, amps, ints, amp_mask, keep_mask, owners, occ_energy, vir_energy, mix):
    td, k_tiles = amp_mask.shape
    rows, kw = amps.shape
    tr = rows // td
    cols = ints.shape[1]
    k_tile = ints.shape[0] // k_tiles
    cap = max(2, 2 * td // no)
    chunk_tiles = max(1, min(td, 128 // tr))
    nc = td // chunk_tiles
    pieces = 2 * nc
    lead, nb, late = 6, 8, ((6, 8, 10, 12), ())
    cfg = (no, nv, td, tr, chunk_tiles, k_tile, lead, nb, late)
    smem = pl.BlockSpec(memory_space=pltpu.SMEM)
    vmem = pl.BlockSpec(memory_space=pltpu.VMEM)
    hbm = pl.BlockSpec(memory_space=pl.ANY)
    ng = no // 2
    own = owners.reshape(1, td)
    keep = keep_mask.reshape(1, td)
    dma = pltpu.SemaphoreType.DMA
    room = (63 << 20) - no * td * tr * cols * 2
    tiles, order = pl.pallas_call(
        functools.partial(ladder_kernel, cfg),
        out_shape=(
            pltpu.VMEM((no, td, tr, cols), jnp.bfloat16),
            pltpu.VMEM((no, td + 1), jnp.int32),
        ),
        in_specs=[hbm] * 8,
        out_specs=(vmem, hbm),
        scratch_shapes=[
            pltpu.SMEM((k_tiles, td), jnp.int32),
            pltpu.SMEM((1, td), jnp.int32),
            pltpu.SMEM((1, td), jnp.int32),
            pltpu.VMEM((rows // 128, 128), jnp.bfloat16),
            pltpu.VMEM((1, cols), jnp.float32),
            pltpu.VMEM((nv, rows, kw), jnp.bfloat16),
            pltpu.VMEM(ints.shape, jnp.bfloat16),
            pltpu.VMEM(ints.shape, jnp.bfloat16),
            pltpu.VMEM((2, nv, chunk_tiles * tr, kw), jnp.bfloat16),
            pltpu.VMEM((rows, 128), jnp.float32),
            pltpu.VMEM((td, tr, cols), jnp.bfloat16),
            pltpu.VMEM((no, tr, tr), jnp.bfloat16),
            pltpu.VMEM((no, 1, td), jnp.int32),
            pltpu.SMEM((no, 1, td), jnp.int32),
            pltpu.SMEM((no, td + 1), jnp.int32),
            pltpu.VMEM((1, cols), jnp.float32),
            pltpu.VMEM((1, td), jnp.int32),
            pltpu.SMEM((1, td), jnp.int32),
            dma((12,)),
            dma((nv - 4, nc)),
            dma((4, pieces)),
            dma((3, nv)),
            dma((no, nb)),
            dma((1,)),
            dma((ng,)),
            dma((ng,)),
            dma((no, nc + 1)),
            dma((ng,)),
            dma((ng,)),
            dma((1,)),
            dma((2, no)),
            dma((2, no)),
            dma((2,)),
            dma((2,)),
        ],
        compiler_params=pltpu.CompilerParams(
            collective_id=0, has_side_effects=True, vmem_limit_bytes=room
        ),
    )(
        amps, ints, amp_mask.T, keep, own, occ_energy.reshape(rows // 128, 128),
        vir_energy.reshape(1, cols), mix,
    )
    return pl.pallas_call(
        functools.partial(place_kernel, cap),
        out_shape=jax.ShapeDtypeStruct((no * cap, tr, cols), jnp.bfloat16),
        in_specs=[smem, vmem],
        out_specs=hbm,
        scratch_shapes=[pltpu.VMEM((tr, cols), jnp.bfloat16), dma],
        compiler_params=pltpu.CompilerParams(vmem_limit_bytes=24 * 1024 * 1024),
    )(order, tiles)


def solution(mesh):
    in_specs = (
        P("occ", "vir"),
        P(None, "vir"),
        P("occ", None),
        P("occ", "vir"),
        P("occ", None),
        P("occ"),
        P("vir"),
        P("occ", None, None),
    )
    body = functools.partial(shards, mesh.shape["occ"], mesh.shape["vir"])
    return jax.shard_map(
        body, mesh=mesh, in_specs=in_specs, out_specs=P("occ", None, "vir"), check_vma=False
    )
```

```python
import functools
import operator

import jax
import jax.numpy as jnp
from jax import lax
from jax.experimental import pallas as pl
from jax.experimental.pallas import tpu as pltpu
from jax.sharding import PartitionSpec as P

MESH = pl.DeviceIdType.MESH


def ladder_kernel(
    cfg, amps, ints, amp_mask_in, keep_in, own_in, occ_in, vir_in, mix, tiles, order,
    amp_mask, keep, own_s, occ, vir, gath, ints_own, ints_end, masked, occ_col, tiles_end, mix_all, own_all, own_tab, nxt, placed,
    vir_end, keep_land, keep_end,
    lsem, rsem_n, rsem_e, ssem_g, rsem_b, ssem_b, ssem_bx, ssem_bc, rsem_t, ssem_c, ssem_t, ssem_r,
    rsem_o, ssem_o, rsem_s, ssem_s,
):
    no, nv, td, tr, chunk_tiles, k_tile, lead, nb, late = cfg
    ng, nz = no // 2, nv // 2
    rows, kw = amps.shape
    depth, cols = ints.shape
    cr = chunk_tiles * tr
    nc = rows // cr
    pt = chunk_tiles // 2
    pr = pt * tr
    np_ = rows // pr
    share = depth // no
    part = share // nb
    o, v = lax.axis_index("occ"), lax.axis_index("vir")
    g, c = o // 2, o % 2
    z, y = v // 2, v % 2
    mate = z * 2 + (1 - y)
    is_end = (z == 0) | (z == nz - 1)
    inner = jnp.logical_not(is_end)
    has_end = (z == 1) | (z == nz - 2)
    go_up = (z >= 1) & (z < nz - 2)
    go_down = (z > 1) & (z <= nz - 2)
    partner = {"occ": g * 2 + (1 - c), "vir": v}
    side = {"occ": o, "vir": mate}
    above = {"occ": o, "vir": (z + 1) * 2 + y}
    below = {"occ": o, "vir": (z - 1) * 2 + y}
    inward = {"occ": o, "vir": jnp.where(z == 0, 1, nz - 2) * 2 + y}
    outward = {"occ": o, "vir": jnp.where(z == 1, 0, nz - 1) * 2 + y}

    barrier = pltpu.get_barrier_semaphore()

    def greet(device):
        pl.semaphore_signal(barrier, inc=1, device_id=device, device_id_type=MESH)

    for d in range(1, no):
        greet({"occ": (o + d) % no, "vir": v})
    greet(side)

    @pl.when(z < nz - 1)
    def _():
        greet(above)

    @pl.when(z > 0)
    def _():
        greet(below)

    load_own = pltpu.make_async_copy(own_in, own_all.at[o], lsem.at[0])
    load_mix = pltpu.make_async_copy(mix.at[0], mix_all.at[o], lsem.at[1])
    load_ints = pltpu.make_async_copy(ints, ints_own, lsem.at[2])
    load_amps = pltpu.make_async_copy(amps, gath.at[v], lsem.at[3])
    loads = [
        pltpu.make_async_copy(src, dst, lsem.at[7 + n])
        for n, (src, dst) in enumerate(
            ((amp_mask_in, amp_mask), (keep_in, keep), (own_in, own_s), (occ_in, occ), (vir_in, vir)))
    ]
    load_own.start()
    load_mix.start()

    @pl.when(inner)
    def _():
        for copy in loads:
            copy.start()
        load_amps.start()
        load_ints.start()

    both = jnp.where(z < nz - 1, 1, 0) + jnp.where(z > 0, 1, 0)
    pl.semaphore_wait(barrier, no + both)

    at_both, at_first = late if nz == 4 else (late[0], ())

    def among(i, pieces):
        return functools.reduce(operator.or_, [i == q for q in pieces], i < 0)

    def crosses_early(i):
        return jnp.logical_not(among(i, at_both + at_first))

    early = (np_ - len(at_both) - len(at_first)) * pr

    def piece(src, slot, far, i, send_sem, device):
        window = pl.ds(pl.multiple_of(i * pr, pr), pr)
        return pltpu.make_async_remote_copy(
            src_ref=src.at[window], dst_ref=gath.at[slot, window], send_sem=send_sem,
            recv_sem=rsem_e.at[far, i], device_id=device, device_id_type=MESH,
        )

    def chunk(src, slot, i, send_sem, device):
        window = pl.ds(pl.multiple_of(i * cr, cr), cr)
        return pltpu.make_async_remote_copy(
            src_ref=src.at[window], dst_ref=gath.at[slot, window], send_sem=send_sem,
            recv_sem=rsem_n.at[slot - 2, i], device_id=device, device_id_type=MESH,
        )

    def arrive(slot, far, i):
        piece(gath.at[slot], slot, far, i, ssem_g.at[2, 0], side).wait_recv()

    def arrive_chunk(slot, i):
        chunk(gath.at[slot], slot, i, ssem_g.at[2, 0], side).wait_recv()

    def small(d, o2):
        peer = {"occ": (o + d) % no, "vir": v}
        return [
            pltpu.make_async_remote_copy(
                src_ref=own_in, dst_ref=own_all.at[o2], send_sem=ssem_o.at[0, d],
                recv_sem=rsem_o.at[0, o2], device_id=peer, device_id_type=MESH),
            pltpu.make_async_remote_copy(
                src_ref=mix.at[0], dst_ref=mix_all.at[o2], send_sem=ssem_o.at[1, d],
                recv_sem=rsem_o.at[1, o2], device_id=peer, device_id_type=MESH),
        ]

    def end_rows():
        return [
            pltpu.make_async_remote_copy(
                src_ref=vir_in, dst_ref=vir_end, send_sem=ssem_s.at[0], recv_sem=rsem_s.at[0],
                device_id=inward, device_id_type=MESH),
            pltpu.make_async_remote_copy(
                src_ref=keep_in, dst_ref=keep_land, send_sem=ssem_s.at[1], recv_sem=rsem_s.at[1],
                device_id=inward, device_id_type=MESH),
        ]

    def table():
        for d in range(1, no):
            for copy in small(d, (o + d) % no):
                copy.wait_recv()
        load_own.wait()
        load_mix.wait()
        copy = pltpu.make_async_copy(own_all, own_tab, lsem.at[4])
        copy.start()
        copy.wait()

        def scan_source(s, carry):
            nxt[s, td] = td

            def back(n, following):
                t = td - 1 - n
                following = jnp.where(own_tab[s, 0, t] == o, t, following)
                nxt[s, t] = following
                return following

            lax.fori_loop(0, td, back, jnp.int32(td))

            def place(k, position):
                t = nxt[s, position]
                placed[s, k] = t
                return jnp.minimum(t + 1, td)

            lax.fori_loop(0, order.shape[1], place, jnp.int32(0))
            return carry

        lax.fori_loop(0, no, scan_source, 0)
        copy = pltpu.make_async_copy(placed, order, lsem.at[6])
        copy.start()
        copy.wait()

    def group_of(d):
        return ((g + d) % ng) * 2

    def tile_window(p):
        if isinstance(p, int) and p >= nc - 1:
            return pl.ds((nc - 1) * chunk_tiles + (p - nc + 1) * pt, pt)
        return pl.ds(p * chunk_tiles, chunk_tiles)

    def tile_piece(o2, i, send_sem, device):
        window = tile_window(i)
        return pltpu.make_async_remote_copy(
            src_ref=tiles.at[o2, window], dst_ref=tiles.at[o2, window], send_sem=send_sem,
            recv_sem=rsem_t.at[o2, i], device_id=device, device_id_type=MESH,
        )

    def back_piece(i):
        window = tile_window(i)
        return pltpu.make_async_remote_copy(
            src_ref=tiles_end.at[window], dst_ref=tiles.at[o, window], send_sem=ssem_r.at[0],
            recv_sem=rsem_t.at[o, i], device_id=outward, device_id_type=MESH,
        )

    def share_out(i):
        for d in range(1, ng):
            tile_piece(o, i, ssem_t.at[d], {"occ": group_of(d) + c, "vir": v}).start()
        tile_piece(o, i, ssem_c.at[0], partner).start()

    def hand_on(i):
        for d in range(1, ng):
            o2 = group_of(d) + c
            tile_piece(o2, i, ssem_c.at[d], partner).wait_recv()
            tile_piece(o2, i, ssem_c.at[d], partner).start()

    def block(q, p):
        return pl.ds(pl.multiple_of(q * share + p * part, part), part)

    def ints_piece(src, q, p, send_sem, device):
        return pltpu.make_async_remote_copy(
            src_ref=src.at[block(q, p)], dst_ref=ints_end.at[block(q, p)], send_sem=send_sem,
            recv_sem=rsem_b.at[q, p], device_id=device, device_id_type=MESH,
        )

    def ints_arrive(q, p):
        ints_piece(ints_end, q, p, ssem_b.at[0], partner).wait_recv()

    @pl.when(is_end)
    def _():
        own_far = z // (nz - 1) * 2 + y
        mate_far = z // (nz - 1) * 2 + (1 - y)
        for copy in end_rows():
            copy.start()

        def cross(i, carry):
            @pl.when(crosses_early(i))
            def _():
                piece(amps, v, own_far, i, ssem_g.at[2, v], side).start()

            return carry

        lax.fori_loop(0, np_, cross, 0)

        def send_ints(p):
            ints_piece(ints, o, p, ssem_b.at[0], inward).start()

        def send_amps(i):
            piece(amps, v, own_far, i, ssem_g.at[0, v], inward).start()

            @pl.when(crosses_early(i))
            def _():
                arrive(mate, mate_far, i)
                piece(gath.at[mate], mate, mate_far, i, ssem_g.at[0, mate], inward).start()

        for p in range(nb - 1):
            send_ints(p)
        for d in range(1, no):
            for copy in small(d, o):
                copy.start()
        send_amps(0)
        send_ints(nb - 1)

        def rest(i, carry):
            send_amps(i)
            return carry

        lax.fori_loop(1, np_, rest, 0)
        table()

        def pass_on(i):
            tile_piece(o, i, ssem_c.at[0], partner).wait_recv()
            share_out(i)

        def passing(i, carry):
            pass_on(i)

            @pl.when(i >= 2)
            def _():
                hand_on(i - 2)

            return carry

        lax.fori_loop(0, nc - 1, passing, 0)
        for i in (nc - 1, nc):
            pass_on(i)
        for i in (nc - 3, nc - 2, nc - 1, nc):
            hand_on(i)

    def mask_rows(i, tiles_in):
        first = pl.multiple_of(i * cr + tiles_in[0] * tr, tr)
        for slot in range(nv):
            rows_in = gath[slot, pl.ds(first, len(tiles_in) * tr), :]
            column = slot * kw + lax.broadcasted_iota(jnp.int32, (1, kw), 1)
            low, high = slot * kw // k_tile, ((slot + 1) * kw - 1) // k_tile
            for place, n in enumerate(tiles_in):
                t = i * chunk_tiles + n
                flag = jnp.full((1, kw), amp_mask[low, t].astype(jnp.float32))
                for s in range(low + 1, high + 1):
                    flag = jnp.where(column >= s * k_tile, amp_mask[s, t].astype(jnp.float32), flag)
                flag = jnp.broadcast_to(flag, (tr, kw)).astype(jnp.bfloat16)
                masked[i % 2, slot, n * tr:(n + 1) * tr, :] = rows_in[place * tr:(place + 1) * tr] * flag

    def ladder_of(i, tiles_in, right):
        held = pl.ds(tiles_in[0] * tr, len(tiles_in) * tr)
        if kw % 128 == 0:
            left = jnp.concatenate([masked[i % 2, slot, held, :] for slot in range(nv)], axis=1)
            return jnp.dot(left, right[...], preferred_element_type=jnp.float32)
        total = jnp.zeros((len(tiles_in) * tr, cols), jnp.float32)
        for slot in range(nv):
            total += jnp.dot(
                masked[i % 2, slot, held, :], right[slot * kw:(slot + 1) * kw, :],
                preferred_element_type=jnp.float32)
        return total

    every = range(chunk_tiles)
    halves = [range(h * pt, (h + 1) * pt) for h in range(2)]

    def update(i, tiles_in, right, keep_row, vir_row, store, send):
        ladder = ladder_of(i, tiles_in, right).astype(jnp.bfloat16)
        for place, n in enumerate(tiles_in):
            t = i * chunk_tiles + n
            kept = ladder[place * tr:(place + 1) * tr] * keep_row[0, t].astype(jnp.float32).astype(jnp.bfloat16)
            mixed = jnp.dot(mix_all[own_s[0, t]], kept, preferred_element_type=jnp.float32)
            energy = occ_col[pl.ds(pl.multiple_of(t * tr, tr), tr), :]
            denominator = vir_row[...] - jnp.concatenate([energy] * (cols // 128), axis=1)
            store(t, (mixed / denominator).astype(jnp.bfloat16))
            if isinstance(i, int) and i == nc - 1:
                if n % pt == pt - 1:
                    send(i + n // pt)
            elif n == chunk_tiles - 1:
                send(i)

    @pl.when(inner)
    def _():
        def send_own(i):
            @pl.when(go_up)
            def _():
                chunk(amps, v, i, ssem_g.at[0, v], above).start()

            @pl.when(go_down)
            def _():
                chunk(amps, v, i, ssem_g.at[1, v], below).start()

        def send_side(i):
            chunk(amps, v, i, ssem_g.at[2, v], side).start()

        def all_own(i, carry):
            send_own(i)
            send_side(i)
            return carry

        lax.fori_loop(0, nc, all_own, 0)
        for d in range(1, no):
            for copy in small(d, o):
                copy.start()

        for copy in loads:
            copy.wait()
        lanes = occ.shape[1]
        for r in range(occ.shape[0]):
            row = jnp.broadcast_to(occ[...].astype(jnp.float32)[r:r + 1], (128, lanes))
            occ_col[r * lanes:(r + 1) * lanes, :] = jnp.transpose(row)

        def within(i, count, body):
            @pl.when((i >= 0) & (i < count))
            def _():
                body(i)

        def relay(copy, slot, up):
            ok, sem, device = (go_up, 0, above) if up else (go_down, 1, below)

            @pl.when(ok)
            def _():
                copy(ssem_g.at[sem, slot], device).start()

        def from_inner(j, i):
            for near, up in ((z - j, True), (z + j, False)):
                @pl.when((near >= 1) & (near <= nz - 2))
                def _():
                    slot = near * 2 + y
                    arrive_chunk(slot, i)
                    relay(functools.partial(chunk, gath.at[slot], slot, i), slot, up)
                    chunk(gath.at[slot], slot, i, ssem_g.at[2, slot], side).start()

        def from_end(j, i):
            for near, end, first, up in ((z - j, 0, 0, True), (z + j, nz - 1, 2, False)):
                @pl.when(near == end)
                def _():
                    slot = end * 2 + y
                    other = end * 2 + (1 - y)
                    arrive(slot, first + y, i)
                    relay(functools.partial(piece, gath.at[slot], slot, first + y, i), slot, up)

                    @pl.when(crosses_early(i))
                    def _():
                        arrive(other, first + (1 - y), i)
                        relay(functools.partial(piece, gath.at[other], other, first + (1 - y), i), other, up)

                    @pl.when(jnp.logical_not(crosses_early(i)))
                    def _():
                        piece(gath.at[slot], slot, first + y, i, ssem_g.at[2, slot], side).start()

        def from_outward(p):
            @pl.when(has_end)
            def _():
                ints_arrive(o, p)
                for d in range(1, ng):
                    ints_piece(ints_end, o, p, ssem_bx.at[d], {"occ": group_of(d) + c, "vir": v}).start()
                ints_piece(ints_end, o, p, ssem_bc.at[0], partner).start()

        def ints_on(p):
            @pl.when(has_end)
            def _():
                for d in range(1, ng):
                    ints_arrive(group_of(d) + c, p)
                    ints_piece(ints_end, group_of(d) + c, p, ssem_bc.at[d], partner).start()

        def ints_last():
            for p in range(nb):
                for d in range(ng):
                    ints_arrive(group_of(d) + (1 - c), p)

        def compute_end(i, tiles_in=every):
            if tiles_in[0] == 0:
                for zz in range(1, nz - 1):
                    arrive_chunk(zz * 2 + (1 - y), i)
            for q in range(2 * i + tiles_in[0] // pt, 2 * i + tiles_in[-1] // pt + 1) if isinstance(i, int) else (2 * i, 2 * i + 1):
                if nz == 4:
                    near, far = z - 1, 2 - z

                    @pl.when(among(q, at_both))
                    def _():
                        arrive(near * 6 + 1 - y, near * 2 + 1 - y, q)

                    @pl.when(jnp.logical_not(among(q, at_both)))
                    def _():
                        arrive(far * 6 + y, far * 2 + y, q)

                    arrive(far * 6 + 1 - y, far * 2 + 1 - y, q)
                else:
                    @pl.when(jnp.logical_not(crosses_early(q)))
                    def _():
                        arrive(1 - y, 1 - y, q)
                        arrive((nz - 1) * 2 + (1 - y), 2 + (1 - y), q)

            mask_rows(i, tiles_in)

            @pl.when(has_end)
            def _():
                if not (isinstance(i, int) and i):
                    @pl.when(i == 0)
                    def _():
                        ints_last()

                def store_end(t, value):
                    tiles_end[t] = value

                update(i, tiles_in, ints_end, keep_end, vir_end, store_end, lambda q: back_piece(q).start())

        def compute_own(i):
            def store_own(t, value):
                tiles[o, t] = value

            update(i, every, ints_own, keep, vir, store_own, share_out)

            if isinstance(i, int):
                if i >= 2:
                    hand_on(i - 2)
            else:
                @pl.when(i >= 2)
                def _():
                    hand_on(i - 2)

        b_in = {0: (0,), 1: (1,), 2: (2,), 3: (3,), 4: (4,), 5: (5,), 6: (6,), 7: (7,)}
        b_on = {3: (0,), 4: (1,), 5: (2,), 6: (3,), 7: (4, 5), 8: (6, 7)}
        lag = 2 * (nz - 3) + 2
        assert nz >= 4 and np_ == 2 * nc

        def near_part(n):
            for j in range(1, nz - 2):
                within(n - (j - 1), nc, functools.partial(from_inner, j))

        def parts_at(s, events, body):
            for at, parts in events.items():
                @pl.when(s == at)
                def _():
                    for p in parts:
                        body(p)

        def before(s):
            parts_at(s, b_in, from_outward)

            @pl.when(s == 2)
            def _():
                load_ints.wait()
                load_amps.wait()
                table()

                @pl.when(has_end)
                def _():
                    for copy in end_rows():
                        copy.wait_recv()
                    copy = pltpu.make_async_copy(keep_land, keep_end, lsem.at[5])
                    copy.start()
                    copy.wait()

        def ends_part(e):
            near, far = z - 1, 2 - z
            across = {"occ": o, "vir": (3 - z) * 2 + y}

            def to_across(slot, far_slot, i):
                piece(gath.at[slot], slot, far_slot, i, ssem_g.at[near, slot], across).start()

            def to_side(slot, far_slot, i):
                piece(gath.at[slot], slot, far_slot, i, ssem_g.at[2, slot], side).start()

            def first(i):
                slot, other = near * 6 + y, near * 6 + 1 - y
                arrive(slot, near * 2 + y, i)
                to_across(slot, near * 2 + y, i)

                @pl.when(crosses_early(i))
                def _():
                    arrive(other, near * 2 + 1 - y, i)
                    to_across(other, near * 2 + 1 - y, i)

                @pl.when(jnp.logical_not(crosses_early(i)))
                def _():
                    to_side(slot, near * 2 + y, i)

            def second(i):
                slot, other = far * 6 + y, near * 6 + 1 - y

                @pl.when(among(i, at_both))
                def _():
                    arrive(slot, far * 2 + y, i)
                    to_side(slot, far * 2 + y, i)

                @pl.when(among(i, at_first))
                def _():
                    arrive(other, near * 2 + 1 - y, i)
                    to_across(other, near * 2 + 1 - y, i)

            within(e, np_, first)
            within(e - 2, np_, second)

        def far_part(e):
            if nz == 4:
                ends_part(e)
                return
            for j in range(1, nz - 1):
                within(e - 2 * (j - 1), np_, functools.partial(from_end, j))

        def loop(low, high, body):
            def one(i, carry):
                body(i)
                return carry

            lax.fori_loop(low, high, one, 0)

        if nz == 4:
            def opening(s):
                near_part(s)
                before(s)
                parts_at(s, b_on, ints_on)

            def early_step(e):
                near_part(lead + e)
                before(lead + e)
                far_part(e)
                parts_at(lead + e, b_on, ints_on)


            def pair(k):
                far_part(2 * k + 4)
                compute_end(k)
                far_part(2 * k + 5)
                compute_own(k)

            loop(0, lead, opening)
            loop(0, 4, early_step)
            loop(0, nc - 2, pair)
            compute_end(nc - 2)
            compute_own(nc - 2)
            for half in halves:
                compute_end(nc - 1, half)
            compute_own(nc - 1)
        else:
            def step(s):
                near_part(s)
                before(s)
                e = s - lead
                far_part(e)
                parts_at(s, b_on, ints_on)

                @pl.when((e > lag) & ((e - lag) % 2 == 1) & (e < lag + 2 * nc - 2))
                def _():
                    k = (e - lag - 1) // 2
                    compute_end(k)
                    compute_own(k)

            loop(0, lead + np_ + lag, step)
            compute_end(nc - 1)
            compute_own(nc - 1)

        for i in (nc - 2, nc - 1, nc):
            hand_on(i)

    def last(i, carry):
        for d in range(ng):
            tile_piece(group_of(d) + (1 - c), i, ssem_c.at[d], partner).wait_recv()
        return carry

    lax.fori_loop(0, nc - 1, last, 0)
    for i in (nc - 1, nc):
        last(i, 0)

    def sent(whole, send_sem, recv_sem):
        pltpu.make_async_remote_copy(
            src_ref=whole, dst_ref=whole, send_sem=send_sem, recv_sem=recv_sem,
            device_id=partner, device_id_type=MESH).wait_send()

    def sent_rows(count, direction, slot):
        if count:
            sent(gath.at[0, pl.ds(0, count)], ssem_g.at[direction, slot], rsem_e.at[0, 0])

    @pl.when(is_end)
    def _():
        sent_rows(early, 2, v)
        sent_rows(rows, 0, v)
        sent_rows(early, 0, mate)
        sent(ints_end.at[pl.ds(0, share)], ssem_b.at[0], rsem_b.at[0, 0])
        for copy in end_rows():
            copy.wait_send()

    @pl.when(inner)
    def _():
        sent_rows(rows, 2, v)
        for zz in range(nz):
            is_far = zz in (0, nz - 1)
            for direction, ok, along in ((0, go_up, zz <= z), (1, go_down, zz >= z)):
                @pl.when(ok & along)
                def _():
                    sent_rows(rows, direction, zz * 2 + y)
                    if is_far:
                        sent_rows(early + len(at_first) * pr, direction, zz * 2 + (1 - y))

            @pl.when(zz != z)
            def _():
                sent_rows(len(at_both) * pr if is_far else rows, 2, zz * 2 + y)

            if is_far and at_first:
                @pl.when(z == (1 if zz == 0 else nz - 2))
                def _():
                    sent_rows(len(at_first) * pr, 2, zz * 2 + y)

        @pl.when(has_end)
        def _():
            for d in range(ng):
                whole = ints_end.at[pl.ds(0, share)]
                sent(whole, ssem_bc.at[d], rsem_b.at[0, 0])
                if d:
                    sent(whole, ssem_bx.at[d], rsem_b.at[0, 0])
            sent(tiles_end, ssem_r.at[0], rsem_t.at[0, 0])

    for d in range(ng):
        sent(tiles.at[d], ssem_c.at[d], rsem_t.at[0, 0])
        if d:
            sent(tiles.at[d], ssem_t.at[d], rsem_t.at[0, 0])
    for d in range(1, no):
        for copy in small(d, o):
            copy.wait_send()


def place_kernel(cap, order, tiles, out, blank, sem):
    no, td = tiles.shape[:2]
    blank[...] = jnp.zeros_like(blank)

    def source(s, carry):
        for k in range(cap):
            t = order[s, k]

            @pl.when(t < td)
            def _():
                pltpu.make_async_copy(tiles.at[s, t], out.at[s * cap + k], sem).start()

            @pl.when(t >= td)
            def _():
                pltpu.make_async_copy(blank, out.at[s * cap + k], sem).start()

        return carry

    lax.fori_loop(0, no, source, 0)
    pltpu.make_async_copy(out, out, sem).wait()


def shards(no, nv, amps, ints, amp_mask, keep_mask, owners, occ_energy, vir_energy, mix):
    td, k_tiles = amp_mask.shape
    rows, kw = amps.shape
    tr = rows // td
    cols = ints.shape[1]
    k_tile = ints.shape[0] // k_tiles
    cap = max(2, 2 * td // no)
    chunk_tiles = max(1, min(td, 128 // tr))
    nc = td // chunk_tiles
    pieces = 2 * nc
    lead, nb, late = 6, 8, ((6, 8, 10, 12), ())
    cfg = (no, nv, td, tr, chunk_tiles, k_tile, lead, nb, late)
    smem = pl.BlockSpec(memory_space=pltpu.SMEM)
    vmem = pl.BlockSpec(memory_space=pltpu.VMEM)
    hbm = pl.BlockSpec(memory_space=pl.ANY)
    ng = no // 2
    own = owners.reshape(1, td)
    keep = keep_mask.reshape(1, td)
    dma = pltpu.SemaphoreType.DMA
    room = (63 << 20) - no * td * tr * cols * 2
    tiles, order = pl.pallas_call(
        functools.partial(ladder_kernel, cfg),
        out_shape=(
            pltpu.VMEM((no, td, tr, cols), jnp.bfloat16),
            pltpu.VMEM((no, cap), jnp.int32),
        ),
        in_specs=[hbm] * 8,
        out_specs=(vmem, hbm),
        scratch_shapes=[
            pltpu.SMEM((k_tiles, td), jnp.int32),
            pltpu.SMEM((1, td), jnp.int32),
            pltpu.SMEM((1, td), jnp.int32),
            pltpu.VMEM((rows // 128, 128), jnp.bfloat16),
            pltpu.VMEM((1, cols), jnp.float32),
            pltpu.VMEM((nv, rows, kw), jnp.bfloat16),
            pltpu.VMEM(ints.shape, jnp.bfloat16),
            pltpu.VMEM(ints.shape, jnp.bfloat16),
            pltpu.VMEM((2, nv, chunk_tiles * tr, kw), jnp.bfloat16),
            pltpu.VMEM((rows, 128), jnp.float32),
            pltpu.VMEM((td, tr, cols), jnp.bfloat16),
            pltpu.VMEM((no, tr, tr), jnp.bfloat16),
            pltpu.VMEM((no, 1, td), jnp.int32),
            pltpu.SMEM((no, 1, td), jnp.int32),
            pltpu.SMEM((no, td + 1), jnp.int32),
            pltpu.SMEM((no, cap), jnp.int32),
            pltpu.VMEM((1, cols), jnp.float32),
            pltpu.VMEM((1, td), jnp.int32),
            pltpu.SMEM((1, td), jnp.int32),
            dma((12,)),
            dma((nv - 4, nc)),
            dma((4, pieces)),
            dma((3, nv)),
            dma((no, nb)),
            dma((1,)),
            dma((ng,)),
            dma((ng,)),
            dma((no, nc + 1)),
            dma((ng,)),
            dma((ng,)),
            dma((1,)),
            dma((2, no)),
            dma((2, no)),
            dma((2,)),
            dma((2,)),
        ],
        compiler_params=pltpu.CompilerParams(
            collective_id=0, has_side_effects=True, vmem_limit_bytes=room
        ),
    )(
        amps, ints, amp_mask.T, keep, own, occ_energy.reshape(rows // 128, 128),
        vir_energy.reshape(1, cols), mix,
    )
    return pl.pallas_call(
        functools.partial(place_kernel, cap),
        out_shape=jax.ShapeDtypeStruct((no * cap, tr, cols), jnp.bfloat16),
        in_specs=[smem, vmem],
        out_specs=hbm,
        scratch_shapes=[pltpu.VMEM((tr, cols), jnp.bfloat16), dma],
        compiler_params=pltpu.CompilerParams(vmem_limit_bytes=24 * 1024 * 1024),
    )(order, tiles)


def solution(mesh):
    in_specs = (
        P("occ", "vir"),
        P(None, "vir"),
        P("occ", None),
        P("occ", "vir"),
        P("occ", None),
        P("occ"),
        P("vir"),
        P("occ", None, None),
    )
    body = functools.partial(shards, mesh.shape["occ"], mesh.shape["vir"])
    return jax.shard_map(
        body, mesh=mesh, in_specs=in_specs, out_specs=P("occ", None, "vir"), check_vma=False
    )
```

```python
import functools
import operator

import jax
import jax.numpy as jnp
from jax import lax
from jax.experimental import pallas as pl
from jax.experimental.pallas import tpu as pltpu
from jax.sharding import PartitionSpec as P

MESH = pl.DeviceIdType.MESH


def ladder_kernel(
    cfg, amps, ints, amp_mask_in, keep_in, own_in, occ_in, vir_in, mix, tiles, order,
    amp_mask, keep, own_s, occ, vir, gath, ints_own, ints_end, masked, occ_col, tiles_end, mix_all, own_all, own_tab, nxt, placed,
    vir_end, keep_land, keep_end,
    lsem, rsem_n, rsem_e, ssem_g, rsem_b, ssem_b, ssem_bx, ssem_bc, rsem_t, ssem_c, ssem_t, ssem_r,
    rsem_o, ssem_o, rsem_s, ssem_s,
):
    no, nv, td, tr, chunk_tiles, k_tile, lead, nb, late = cfg
    ng, nz = no // 2, nv // 2
    rows, kw = amps.shape
    depth, cols = ints.shape
    cr = chunk_tiles * tr
    nc = rows // cr
    pt = chunk_tiles // 2
    pr = pt * tr
    np_ = rows // pr
    share = depth // no
    part = share // nb
    o, v = lax.axis_index("occ"), lax.axis_index("vir")
    g, c = o // 2, o % 2
    z, y = v // 2, v % 2
    mate = z * 2 + (1 - y)
    is_end = (z == 0) | (z == nz - 1)
    inner = jnp.logical_not(is_end)
    has_end = (z == 1) | (z == nz - 2)
    go_up = (z >= 1) & (z < nz - 2)
    go_down = (z > 1) & (z <= nz - 2)
    partner = {"occ": g * 2 + (1 - c), "vir": v}
    side = {"occ": o, "vir": mate}
    above = {"occ": o, "vir": (z + 1) * 2 + y}
    below = {"occ": o, "vir": (z - 1) * 2 + y}
    inward = {"occ": o, "vir": jnp.where(z == 0, 1, nz - 2) * 2 + y}
    outward = {"occ": o, "vir": jnp.where(z == 1, 0, nz - 1) * 2 + y}

    barrier = pltpu.get_barrier_semaphore()

    def greet(device):
        pl.semaphore_signal(barrier, inc=1, device_id=device, device_id_type=MESH)

    for d in range(1, no):
        greet({"occ": (o + d) % no, "vir": v})
    greet(side)

    @pl.when(z < nz - 1)
    def _():
        greet(above)

    @pl.when(z > 0)
    def _():
        greet(below)

    load_own = pltpu.make_async_copy(own_in, own_all.at[o], lsem.at[0])
    load_mix = pltpu.make_async_copy(mix.at[0], mix_all.at[o], lsem.at[1])
    load_ints = pltpu.make_async_copy(ints, ints_own, lsem.at[2])
    load_amps = pltpu.make_async_copy(amps, gath.at[v], lsem.at[3])
    loads = [
        pltpu.make_async_copy(src, dst, lsem.at[7 + n])
        for n, (src, dst) in enumerate(
            ((amp_mask_in, amp_mask), (keep_in, keep), (own_in, own_s), (occ_in, occ), (vir_in, vir)))
    ]
    load_own.start()
    load_mix.start()

    @pl.when(inner)
    def _():
        for copy in loads:
            copy.start()
        load_amps.start()
        load_ints.start()

    both = jnp.where(z < nz - 1, 1, 0) + jnp.where(z > 0, 1, 0)
    pl.semaphore_wait(barrier, no + both)

    at_both, at_first = late if nz == 4 else (late[0], ())

    def among(i, pieces):
        return functools.reduce(operator.or_, [i == q for q in pieces], i < 0)

    def crosses_early(i):
        return jnp.logical_not(among(i, at_both + at_first))

    early = (np_ - len(at_both) - len(at_first)) * pr

    def piece(src, slot, far, i, send_sem, device):
        window = pl.ds(pl.multiple_of(i * pr, pr), pr)
        return pltpu.make_async_remote_copy(
            src_ref=src.at[window], dst_ref=gath.at[slot, window], send_sem=send_sem,
            recv_sem=rsem_e.at[far, i], device_id=device, device_id_type=MESH,
        )

    def chunk(src, slot, i, send_sem, device):
        window = pl.ds(pl.multiple_of(i * cr, cr), cr)
        return pltpu.make_async_remote_copy(
            src_ref=src.at[window], dst_ref=gath.at[slot, window], send_sem=send_sem,
            recv_sem=rsem_n.at[slot - 2, i], device_id=device, device_id_type=MESH,
        )

    def arrive(slot, far, i):
        piece(gath.at[slot], slot, far, i, ssem_g.at[2, 0], side).wait_recv()

    def arrive_chunk(slot, i):
        chunk(gath.at[slot], slot, i, ssem_g.at[2, 0], side).wait_recv()

    def small(d, o2):
        peer = {"occ": (o + d) % no, "vir": v}
        return [
            pltpu.make_async_remote_copy(
                src_ref=own_in, dst_ref=own_all.at[o2], send_sem=ssem_o.at[0, d],
                recv_sem=rsem_o.at[0, o2], device_id=peer, device_id_type=MESH),
            pltpu.make_async_remote_copy(
                src_ref=mix.at[0], dst_ref=mix_all.at[o2], send_sem=ssem_o.at[1, d],
                recv_sem=rsem_o.at[1, o2], device_id=peer, device_id_type=MESH),
        ]

    def end_rows():
        return [
            pltpu.make_async_remote_copy(
                src_ref=vir_in, dst_ref=vir_end, send_sem=ssem_s.at[0], recv_sem=rsem_s.at[0],
                device_id=inward, device_id_type=MESH),
            pltpu.make_async_remote_copy(
                src_ref=keep_in, dst_ref=keep_land, send_sem=ssem_s.at[1], recv_sem=rsem_s.at[1],
                device_id=inward, device_id_type=MESH),
        ]

    def table():
        for d in range(1, no):
            for copy in small(d, (o + d) % no):
                copy.wait_recv()
        load_own.wait()
        load_mix.wait()
        copy = pltpu.make_async_copy(own_all, own_tab, lsem.at[4])
        copy.start()
        copy.wait()

        def scan_source(s, carry):
            nxt[s, td] = td

            def back(n, following):
                t = td - 1 - n
                following = jnp.where(own_tab[s, 0, t] == o, t, following)
                nxt[s, t] = following
                return following

            lax.fori_loop(0, td, back, jnp.int32(td))

            def place(k, position):
                t = nxt[s, position]
                placed[s, k] = t
                return jnp.minimum(t + 1, td)

            lax.fori_loop(0, order.shape[1], place, jnp.int32(0))
            return carry

        lax.fori_loop(0, no, scan_source, 0)
        copy = pltpu.make_async_copy(placed, order, lsem.at[6])
        copy.start()
        copy.wait()

    def group_of(d):
        return ((g + d) % ng) * 2

    def tile_window(p):
        if isinstance(p, int) and p >= nc - 1:
            return pl.ds((nc - 1) * chunk_tiles + (p - nc + 1) * pt, pt)
        return pl.ds(p * chunk_tiles, chunk_tiles)

    def tile_piece(o2, i, send_sem, device):
        window = tile_window(i)
        return pltpu.make_async_remote_copy(
            src_ref=tiles.at[o2, window], dst_ref=tiles.at[o2, window], send_sem=send_sem,
            recv_sem=rsem_t.at[o2, i], device_id=device, device_id_type=MESH,
        )

    def back_piece(i):
        window = tile_window(i)
        return pltpu.make_async_remote_copy(
            src_ref=tiles_end.at[window], dst_ref=tiles.at[o, window], send_sem=ssem_r.at[0],
            recv_sem=rsem_t.at[o, i], device_id=outward, device_id_type=MESH,
        )

    def share_out(i):
        for d in range(1, ng):
            tile_piece(o, i, ssem_t.at[d], {"occ": group_of(d) + c, "vir": v}).start()
        tile_piece(o, i, ssem_c.at[0], partner).start()

    def hand_on(i):
        for d in range(1, ng):
            o2 = group_of(d) + c
            tile_piece(o2, i, ssem_c.at[d], partner).wait_recv()
            tile_piece(o2, i, ssem_c.at[d], partner).start()

    def block(q, p):
        return pl.ds(pl.multiple_of(q * share + p * part, part), part)

    def ints_piece(src, q, p, send_sem, device):
        return pltpu.make_async_remote_copy(
            src_ref=src.at[block(q, p)], dst_ref=ints_end.at[block(q, p)], send_sem=send_sem,
            recv_sem=rsem_b.at[q, p], device_id=device, device_id_type=MESH,
        )

    def ints_arrive(q, p):
        ints_piece(ints_end, q, p, ssem_b.at[0], partner).wait_recv()

    @pl.when(is_end)
    def _():
        own_far = z // (nz - 1) * 2 + y
        mate_far = z // (nz - 1) * 2 + (1 - y)
        for copy in end_rows():
            copy.start()

        def cross(i, carry):
            @pl.when(crosses_early(i))
            def _():
                piece(amps, v, own_far, i, ssem_g.at[2, v], side).start()

            return carry

        lax.fori_loop(0, np_, cross, 0)

        def send_ints(p):
            ints_piece(ints, o, p, ssem_b.at[0], inward).start()

        def send_amps(i):
            piece(amps, v, own_far, i, ssem_g.at[0, v], inward).start()

            @pl.when(crosses_early(i))
            def _():
                arrive(mate, mate_far, i)
                piece(gath.at[mate], mate, mate_far, i, ssem_g.at[0, mate], inward).start()

        for p in range(nb - 1):
            send_ints(p)
        for d in range(1, no):
            for copy in small(d, o):
                copy.start()
        send_amps(0)
        send_ints(nb - 1)

        def rest(i, carry):
            send_amps(i)
            return carry

        lax.fori_loop(1, np_, rest, 0)
        table()

        def pass_on(i):
            tile_piece(o, i, ssem_c.at[0], partner).wait_recv()
            share_out(i)

        def passing(i, carry):
            pass_on(i)

            @pl.when(i >= 2)
            def _():
                hand_on(i - 2)

            return carry

        lax.fori_loop(0, nc - 1, passing, 0)
        for i in (nc - 1, nc):
            pass_on(i)
        for i in (nc - 3, nc - 2, nc - 1, nc):
            hand_on(i)

    def mask_rows(i, tiles_in):
        first = pl.multiple_of(i * cr + tiles_in[0] * tr, tr)
        for slot in range(nv):
            rows_in = gath[slot, pl.ds(first, len(tiles_in) * tr), :]
            column = slot * kw + lax.broadcasted_iota(jnp.int32, (1, kw), 1)
            low, high = slot * kw // k_tile, ((slot + 1) * kw - 1) // k_tile
            for place, n in enumerate(tiles_in):
                t = i * chunk_tiles + n
                flag = jnp.full((1, kw), amp_mask[low, t].astype(jnp.float32))
                for s in range(low + 1, high + 1):
                    flag = jnp.where(column >= s * k_tile, amp_mask[s, t].astype(jnp.float32), flag)
                flag = jnp.broadcast_to(flag, (tr, kw)).astype(jnp.bfloat16)
                masked[i % 2, slot, n * tr:(n + 1) * tr, :] = rows_in[place * tr:(place + 1) * tr] * flag

    def ladder_of(i, tiles_in, right):
        held = pl.ds(tiles_in[0] * tr, len(tiles_in) * tr)
        if kw % 128 == 0:
            left = jnp.concatenate([masked[i % 2, slot, held, :] for slot in range(nv)], axis=1)
            return jnp.dot(left, right[...], preferred_element_type=jnp.float32)
        total = jnp.zeros((len(tiles_in) * tr, cols), jnp.float32)
        for slot in range(nv):
            total += jnp.dot(
                masked[i % 2, slot, held, :], right[slot * kw:(slot + 1) * kw, :],
                preferred_element_type=jnp.float32)
        return total

    every = range(chunk_tiles)
    halves = [range(h * pt, (h + 1) * pt) for h in range(2)]

    def update(i, tiles_in, right, keep_row, vir_row, store, send):
        ladder = ladder_of(i, tiles_in, right).astype(jnp.bfloat16)
        for place, n in enumerate(tiles_in):
            t = i * chunk_tiles + n
            kept = ladder[place * tr:(place + 1) * tr] * keep_row[0, t].astype(jnp.float32).astype(jnp.bfloat16)
            mixed = jnp.dot(mix_all[own_s[0, t]], kept, preferred_element_type=jnp.float32)
            energy = occ_col[pl.ds(pl.multiple_of(t * tr, tr), tr), :]
            denominator = vir_row[...] - jnp.concatenate([energy] * (cols // 128), axis=1)
            store(t, (mixed / denominator).astype(jnp.bfloat16))
            if isinstance(i, int) and i == nc - 1:
                if n % pt == pt - 1:
                    send(i + n // pt)
            elif n == chunk_tiles - 1:
                send(i)

    @pl.when(inner)
    def _():
        def send_own(i):
            @pl.when(go_up)
            def _():
                chunk(amps, v, i, ssem_g.at[0, v], above).start()

            @pl.when(go_down)
            def _():
                chunk(amps, v, i, ssem_g.at[1, v], below).start()

        def send_side(i):
            chunk(amps, v, i, ssem_g.at[2, v], side).start()

        def all_own(i, carry):
            send_own(i)
            send_side(i)
            return carry

        lax.fori_loop(0, nc, all_own, 0)
        for d in range(1, no):
            for copy in small(d, o):
                copy.start()

        for copy in loads:
            copy.wait()
        lanes = occ.shape[1]
        for r in range(occ.shape[0]):
            row = jnp.broadcast_to(occ[...].astype(jnp.float32)[r:r + 1], (128, lanes))
            occ_col[r * lanes:(r + 1) * lanes, :] = jnp.transpose(row)

        def within(i, count, body):
            @pl.when((i >= 0) & (i < count))
            def _():
                body(i)

        def relay(copy, slot, up):
            ok, sem, device = (go_up, 0, above) if up else (go_down, 1, below)

            @pl.when(ok)
            def _():
                copy(ssem_g.at[sem, slot], device).start()

        def from_inner(j, i):
            for near, up in ((z - j, True), (z + j, False)):
                @pl.when((near >= 1) & (near <= nz - 2))
                def _():
                    slot = near * 2 + y
                    arrive_chunk(slot, i)
                    relay(functools.partial(chunk, gath.at[slot], slot, i), slot, up)
                    chunk(gath.at[slot], slot, i, ssem_g.at[2, slot], side).start()

        def from_end(j, i):
            for near, end, first, up in ((z - j, 0, 0, True), (z + j, nz - 1, 2, False)):
                @pl.when(near == end)
                def _():
                    slot = end * 2 + y
                    other = end * 2 + (1 - y)
                    arrive(slot, first + y, i)
                    relay(functools.partial(piece, gath.at[slot], slot, first + y, i), slot, up)

                    @pl.when(crosses_early(i))
                    def _():
                        arrive(other, first + (1 - y), i)
                        relay(functools.partial(piece, gath.at[other], other, first + (1 - y), i), other, up)

                    @pl.when(jnp.logical_not(crosses_early(i)))
                    def _():
                        piece(gath.at[slot], slot, first + y, i, ssem_g.at[2, slot], side).start()

        def from_outward(p):
            @pl.when(has_end)
            def _():
                ints_arrive(o, p)
                for d in range(1, ng):
                    ints_piece(ints_end, o, p, ssem_bx.at[d], {"occ": group_of(d) + c, "vir": v}).start()
                ints_piece(ints_end, o, p, ssem_bc.at[0], partner).start()

        def ints_on(p):
            @pl.when(has_end)
            def _():
                for d in range(1, ng):
                    ints_arrive(group_of(d) + c, p)
                    ints_piece(ints_end, group_of(d) + c, p, ssem_bc.at[d], partner).start()

        def ints_last():
            for p in range(nb):
                for d in range(ng):
                    ints_arrive(group_of(d) + (1 - c), p)

        def compute_end(i, tiles_in=every):
            if tiles_in[0] == 0:
                for zz in range(1, nz - 1):
                    arrive_chunk(zz * 2 + (1 - y), i)
            for q in range(2 * i + tiles_in[0] // pt, 2 * i + tiles_in[-1] // pt + 1) if isinstance(i, int) else (2 * i, 2 * i + 1):
                if nz == 4:
                    near, far = z - 1, 2 - z

                    @pl.when(among(q, at_both))
                    def _():
                        arrive(near * 6 + 1 - y, near * 2 + 1 - y, q)

                    @pl.when(jnp.logical_not(among(q, at_both)))
                    def _():
                        arrive(far * 6 + y, far * 2 + y, q)

                    arrive(far * 6 + 1 - y, far * 2 + 1 - y, q)
                else:
                    @pl.when(jnp.logical_not(crosses_early(q)))
                    def _():
                        arrive(1 - y, 1 - y, q)
                        arrive((nz - 1) * 2 + (1 - y), 2 + (1 - y), q)

            mask_rows(i, tiles_in)

            @pl.when(has_end)
            def _():
                if not (isinstance(i, int) and i):
                    @pl.when(i == 0)
                    def _():
                        ints_last()

                def store_end(t, value):
                    tiles_end[t] = value

                update(i, tiles_in, ints_end, keep_end, vir_end, store_end, lambda q: back_piece(q).start())

        def compute_own(i):
            def store_own(t, value):
                tiles[o, t] = value

            update(i, every, ints_own, keep, vir, store_own, share_out)

            if isinstance(i, int):
                if i >= 2:
                    hand_on(i - 2)
            else:
                @pl.when(i >= 2)
                def _():
                    hand_on(i - 2)

        b_in = {0: (0,), 1: (1,), 2: (2,), 3: (3,), 4: (4,), 5: (5,), 6: (6,), 7: (7,)}
        b_on = {3: (0,), 4: (1,), 5: (2,), 6: (3,), 7: (4, 5), 8: (6, 7)}
        lag = 2 * (nz - 3) + 2
        assert nz >= 4 and np_ == 2 * nc

        def near_part(n):
            for j in range(1, nz - 2):
                within(n - (j - 1), nc, functools.partial(from_inner, j))

        def parts_at(s, events, body):
            for at, parts in events.items():
                @pl.when(s == at)
                def _():
                    for p in parts:
                        body(p)

        def before(s):
            parts_at(s, b_in, from_outward)

            @pl.when(s == 2)
            def _():
                load_ints.wait()
                load_amps.wait()
                table()

                @pl.when(has_end)
                def _():
                    for copy in end_rows():
                        copy.wait_recv()
                    copy = pltpu.make_async_copy(keep_land, keep_end, lsem.at[5])
                    copy.start()
                    copy.wait()

        def ends_part(e):
            near, far = z - 1, 2 - z
            across = {"occ": o, "vir": (3 - z) * 2 + y}

            def to_across(slot, far_slot, i):
                piece(gath.at[slot], slot, far_slot, i, ssem_g.at[near, slot], across).start()

            def to_side(slot, far_slot, i):
                piece(gath.at[slot], slot, far_slot, i, ssem_g.at[2, slot], side).start()

            def first(i):
                slot, other = near * 6 + y, near * 6 + 1 - y
                arrive(slot, near * 2 + y, i)
                to_across(slot, near * 2 + y, i)

                @pl.when(crosses_early(i))
                def _():
                    arrive(other, near * 2 + 1 - y, i)
                    to_across(other, near * 2 + 1 - y, i)

                @pl.when(jnp.logical_not(crosses_early(i)))
                def _():
                    to_side(slot, near * 2 + y, i)

            def second(i):
                slot, other = far * 6 + y, near * 6 + 1 - y

                @pl.when(among(i, at_both))
                def _():
                    arrive(slot, far * 2 + y, i)
                    to_side(slot, far * 2 + y, i)

                @pl.when(among(i, at_first))
                def _():
                    arrive(other, near * 2 + 1 - y, i)
                    to_across(other, near * 2 + 1 - y, i)

            within(e, np_, first)
            within(e - 2, np_, second)

        def far_part(e):
            if nz == 4:
                ends_part(e)
                return
            for j in range(1, nz - 1):
                within(e - 2 * (j - 1), np_, functools.partial(from_end, j))

        def loop(low, high, body):
            def one(i, carry):
                body(i)
                return carry

            lax.fori_loop(low, high, one, 0)

        if nz == 4:
            def opening(s):
                near_part(s)
                before(s)
                parts_at(s, b_on, ints_on)

            def early_step(e):
                near_part(lead + e)
                before(lead + e)
                far_part(e)
                parts_at(lead + e, b_on, ints_on)


            def pair(k):
                far_part(2 * k + 4)
                compute_end(k)
                far_part(2 * k + 5)
                compute_own(k)

            loop(0, lead, opening)
            loop(0, 4, early_step)
            loop(0, nc - 2, pair)
            compute_end(nc - 2)
            compute_own(nc - 2)
            for half in halves:
                compute_end(nc - 1, half)
            compute_own(nc - 1)
        else:
            def step(s):
                near_part(s)
                before(s)
                e = s - lead
                far_part(e)
                parts_at(s, b_on, ints_on)

                @pl.when((e > lag) & ((e - lag) % 2 == 1) & (e < lag + 2 * nc - 2))
                def _():
                    k = (e - lag - 1) // 2
                    compute_end(k)
                    compute_own(k)

            loop(0, lead + np_ + lag, step)
            compute_end(nc - 1)
            compute_own(nc - 1)

        for i in (nc - 2, nc - 1, nc):
            hand_on(i)

    def last(i, carry):
        for d in range(ng):
            tile_piece(group_of(d) + (1 - c), i, ssem_c.at[d], partner).wait_recv()
        return carry

    lax.fori_loop(0, nc - 1, last, 0)
    for i in (nc - 1, nc):
        last(i, 0)

    def sent(whole, send_sem, recv_sem):
        pltpu.make_async_remote_copy(
            src_ref=whole, dst_ref=whole, send_sem=send_sem, recv_sem=recv_sem,
            device_id=partner, device_id_type=MESH).wait_send()

    def sent_rows(count, direction, slot):
        if count:
            sent(gath.at[0, pl.ds(0, count)], ssem_g.at[direction, slot], rsem_e.at[0, 0])

    @pl.when(is_end)
    def _():
        sent_rows(early, 2, v)
        sent_rows(rows, 0, v)
        sent_rows(early, 0, mate)
        sent(ints_end.at[pl.ds(0, share)], ssem_b.at[0], rsem_b.at[0, 0])
        for copy in end_rows():
            copy.wait_send()

    @pl.when(inner)
    def _():
        sent_rows(rows, 2, v)
        for zz in range(nz):
            is_far = zz in (0, nz - 1)
            for direction, ok, along in ((0, go_up, zz <= z), (1, go_down, zz >= z)):
                @pl.when(ok & along)
                def _():
                    sent_rows(rows, direction, zz * 2 + y)
                    if is_far:
                        sent_rows(early + len(at_first) * pr, direction, zz * 2 + (1 - y))

            @pl.when(zz != z)
            def _():
                sent_rows(len(at_both) * pr if is_far else rows, 2, zz * 2 + y)

            if is_far and at_first:
                @pl.when(z == (1 if zz == 0 else nz - 2))
                def _():
                    sent_rows(len(at_first) * pr, 2, zz * 2 + y)

        @pl.when(has_end)
        def _():
            for d in range(ng):
                whole = ints_end.at[pl.ds(0, share)]
                sent(whole, ssem_bc.at[d], rsem_b.at[0, 0])
                if d:
                    sent(whole, ssem_bx.at[d], rsem_b.at[0, 0])
            sent(tiles_end, ssem_r.at[0], rsem_t.at[0, 0])

    for d in range(ng):
        sent(tiles.at[d], ssem_c.at[d], rsem_t.at[0, 0])
        if d:
            sent(tiles.at[d], ssem_t.at[d], rsem_t.at[0, 0])
    for d in range(1, no):
        for copy in small(d, o):
            copy.wait_send()


def place_kernel(cap, order, tiles, out, blank, sem):
    no, td = tiles.shape[:2]
    blank[...] = jnp.zeros_like(blank)

    def source(s, carry):
        for k in range(cap):
            t = order[s, k]

            @pl.when(t < td)
            def _():
                pltpu.make_async_copy(tiles.at[s, t], out.at[s * cap + k], sem).start()

            @pl.when(t >= td)
            def _():
                pltpu.make_async_copy(blank, out.at[s * cap + k], sem).start()

        return carry

    lax.fori_loop(0, no, source, 0)
    pltpu.make_async_copy(out, out, sem).wait()


def shards(no, nv, amps, ints, amp_mask, keep_mask, owners, occ_energy, vir_energy, mix):
    td, k_tiles = amp_mask.shape
    rows, kw = amps.shape
    tr = rows // td
    cols = ints.shape[1]
    k_tile = ints.shape[0] // k_tiles
    cap = max(2, 2 * td // no)
    chunk_tiles = max(1, min(td, 128 // tr))
    nc = td // chunk_tiles
    pieces = 2 * nc
    lead, nb, late = 6, 8, ((6, 8, 9, 10), ())
    cfg = (no, nv, td, tr, chunk_tiles, k_tile, lead, nb, late)
    smem = pl.BlockSpec(memory_space=pltpu.SMEM)
    vmem = pl.BlockSpec(memory_space=pltpu.VMEM)
    hbm = pl.BlockSpec(memory_space=pl.ANY)
    ng = no // 2
    own = owners.reshape(1, td)
    keep = keep_mask.reshape(1, td)
    dma = pltpu.SemaphoreType.DMA
    room = (63 << 20) - no * td * tr * cols * 2
    tiles, order = pl.pallas_call(
        functools.partial(ladder_kernel, cfg),
        out_shape=(
            pltpu.VMEM((no, td, tr, cols), jnp.bfloat16),
            pltpu.VMEM((no, cap), jnp.int32),
        ),
        in_specs=[hbm] * 8,
        out_specs=(vmem, hbm),
        scratch_shapes=[
            pltpu.SMEM((k_tiles, td), jnp.int32),
            pltpu.SMEM((1, td), jnp.int32),
            pltpu.SMEM((1, td), jnp.int32),
            pltpu.VMEM((rows // 128, 128), jnp.bfloat16),
            pltpu.VMEM((1, cols), jnp.float32),
            pltpu.VMEM((nv, rows, kw), jnp.bfloat16),
            pltpu.VMEM(ints.shape, jnp.bfloat16),
            pltpu.VMEM(ints.shape, jnp.bfloat16),
            pltpu.VMEM((2, nv, chunk_tiles * tr, kw), jnp.bfloat16),
            pltpu.VMEM((rows, 128), jnp.float32),
            pltpu.VMEM((td, tr, cols), jnp.bfloat16),
            pltpu.VMEM((no, tr, tr), jnp.bfloat16),
            pltpu.VMEM((no, 1, td), jnp.int32),
            pltpu.SMEM((no, 1, td), jnp.int32),
            pltpu.SMEM((no, td + 1), jnp.int32),
            pltpu.SMEM((no, cap), jnp.int32),
            pltpu.VMEM((1, cols), jnp.float32),
            pltpu.VMEM((1, td), jnp.int32),
            pltpu.SMEM((1, td), jnp.int32),
            dma((12,)),
            dma((nv - 4, nc)),
            dma((4, pieces)),
            dma((3, nv)),
            dma((no, nb)),
            dma((1,)),
            dma((ng,)),
            dma((ng,)),
            dma((no, nc + 1)),
            dma((ng,)),
            dma((ng,)),
            dma((1,)),
            dma((2, no)),
            dma((2, no)),
            dma((2,)),
            dma((2,)),
        ],
        compiler_params=pltpu.CompilerParams(
            collective_id=0, has_side_effects=True, vmem_limit_bytes=room
        ),
    )(
        amps, ints, amp_mask.T, keep, own, occ_energy.reshape(rows // 128, 128),
        vir_energy.reshape(1, cols), mix,
    )
    return pl.pallas_call(
        functools.partial(place_kernel, cap),
        out_shape=jax.ShapeDtypeStruct((no * cap, tr, cols), jnp.bfloat16),
        in_specs=[smem, vmem],
        out_specs=hbm,
        scratch_shapes=[pltpu.VMEM((tr, cols), jnp.bfloat16), dma],
        compiler_params=pltpu.CompilerParams(vmem_limit_bytes=24 * 1024 * 1024),
    )(order, tiles)


def solution(mesh):
    in_specs = (
        P("occ", "vir"),
        P(None, "vir"),
        P("occ", None),
        P("occ", "vir"),
        P("occ", None),
        P("occ"),
        P("vir"),
        P("occ", None, None),
    )
    body = functools.partial(shards, mesh.shape["occ"], mesh.shape["vir"])
    return jax.shard_map(
        body, mesh=mesh, in_specs=in_specs, out_specs=P("occ", None, "vir"), check_vma=False
    )
```
